128 devices in a mesh: wide: 32 (over z, y, core), narrow: 4 (over x).
Axes of the slice: x: 4, y: 4, z: 4, core: 2. Of those that a mesh axis runs over, the one named last changes fastest.
Arguments:
- modal_unknowns: float32 [180, 262144], P(None, ('wide', 'narrow')), may hold values from -6 to 6
- timestep_metric_scaling: float32 [3, 262144], P(None, ('wide', 'narrow')), may hold values from 0.15 to 0.45
- surface_measure_quotient: float32 [4, 262144], P(None, ('wide', 'narrow')), may hold values from 0.5 to 1.5
- elastic_directional_derivs: float32 [3, 9, 9], replicated, may hold values from -2 to 2
- predictor_derivatives: float32 [3, 20, 20], replicated, may hold values from -1.25 to 1.25
- interior_gradient_tables: float32 [3, 20, 20], replicated, may hold values from -1.25 to 1.25
- interior_restriction: float32 [4, 10, 20], replicated, may hold values from -1.25 to 1.25
- surface_raise_tables: float32 [4, 20, 10], replicated, may hold values from -2 to 2
- riemann_numerical_tables: float32 [2, 9, 9], replicated, may hold values from -2 to 2
- boundary_polynomials_sampled: float32 [16, 10], replicated, may hold values from -2 to 2
- quadrature_gather_weights: float32 [16, 10], replicated, may hold values from -1.5 to 1.5
- thermal_diffusion_resolvent: float32 [64, 64], replicated, as said below
- hydraulic_diffusion_resolvent: float32 [64, 64], replicated, as said below
- thermal_field: float32 [64, 1048576], P(None, ('wide', 'narrow')), may hold values from -6 to 6
- fluid_load: float32 [64, 1048576], P(None, ('wide', 'narrow')), may hold values from -6 to 6
- earlier_sliding_speed: float32 [1048576], P(('wide', 'narrow')), may hold values from 0.05 to 2
- instant_sensitivity_a: float32 [1048576], P(('wide', 'narrow')), may hold values from 0.2 to 1
- aging_memory_theta: float32 [1048576], P(('wide', 'narrow')), may hold values from 0.2 to 0.8
- outbound_ghost_indices: int32 [6, 65536], P(None, ('wide', 'narrow')), may hold values from 0 to 8191
- boundary_entry_index: int32 [4, 262144], P(None, ('wide', 'narrow')), may hold values from 0 to 11263, as said below
- rupture_side_index: int32 [65536], P(('wide', 'narrow')), may hold values from -1 to 8191, as said below
- rupture_seat_partition: int32 [65536], P(('wide', 'narrow')), may hold values from -1 to 127, as said below
Outputs:
- advanced_unknowns: float32 [180, 262144], P(None, ('wide', 'narrow'))
- new_temperature: float32 [64, 1048576], P(None, ('wide', 'narrow'))
- new_pressure: float32 [64, 1048576], P(None, ('wide', 'narrow'))
- new_rate: float32 [1048576], P(('wide', 'narrow'))
The draws below stay inside these ranges and needn't reach their ends.
Inputs may be any that keep to these rules, and one draw needn't show every extreme that they name: `boundary_entry_index`: points only into lists that exist for the partition: list k of the narrow group for k other than its own narrow index, the lower wide list only if w > 0, the upper only if w < 32 - 1. Slot s of a list is used only below a ragged count of that list; each partition uses one list in full. `rupture_side_index`: distinct faces of the partition; the live slots of a partition come first, the rest are -1 here and in rupture_seat_partition. `rupture_seat_partition`: slots i and i' of one partition share an owner when i // 4 == i' // 4 and have distinct owners otherwise; some partition has all 512 slots live; live counts are skewed, the busiest some three times the mean. `thermal_diffusion_resolvent`: dense with a dominant positive diagonal. `hydraulic_diffusion_resolvent`: dense with a dominant positive diagonal.
All inputs are finite; a program needn't handle non-finite values.
Results may differ from the reference program's by a relative error of at most 0.0003.
Values sent between devices are 32-bit elements; how exact they have to be, the bound alone decides.
No kernel may reach another device: no remote copies, remote signals or barrier semaphores. Data moves between devices by JAX's collectives and lax.ppermute only.
A program may use at most 128 MiB of HBM per device.

```python
import math
import jax
import jax.numpy as jnp
from jax import lax

QUANTS = 9
BASIS = 20
FACE_BASIS = 10
POINTS = 16
DEPTH_SAMPLES = 64
NEWTON = 4
ELEM_DEV = 2048
FAULT_DEV = 512
ELEMS = 262144
HALO_CAP = 512
LISTS = 6
PAIR_CAP = 4
RUPTURE_SITES = 1048576
N_WIDE = 32
N_NARROW = 4
DEVICES = 128


def inverse_table(key, depth_sample_total):
    diag_key, spread_key = jax.random.split(key)
    diagonal = jax.random.uniform(diag_key, (depth_sample_total,), jnp.float32, 0.5, 0.8)
    spread = jax.random.normal(spread_key, (depth_sample_total, depth_sample_total), jnp.float32) * (0.25 / depth_sample_total)
    return spread + jnp.diag(diagonal)


def draw_thermal_diffusion_resolvent(key, part):
    return inverse_table(jax.random.fold_in(key, 11), DEPTH_SAMPLES)


def draw_hydraulic_diffusion_resolvent(key, part):
    return inverse_table(jax.random.fold_in(key, 13), DEPTH_SAMPLES)


def draw_boundary_entry_index(key, part):
    accelerator_roster = N_WIDE * N_NARROW
    face_total = 4 * ELEM_DEV
    list_total = N_NARROW + 2
    subkeys = jax.random.split(jax.random.fold_in(key, 3), 4)
    shuffled = jax.vmap(lambda subkey: jax.random.permutation(subkey, face_total))(jax.random.split(subkeys[0], accelerator_roster))
    inside = jax.random.randint(subkeys[1], (accelerator_roster, face_total), 0, face_total, dtype=jnp.int32)
    counts = jax.random.randint(subkeys[2], (accelerator_roster, list_total), HALO_CAP // 3, HALO_CAP + 1, dtype=jnp.int32)
    device_ids = jnp.arange(accelerator_roster, dtype=jnp.int32)
    wide_index = device_ids // N_NARROW
    narrow_index = device_ids % N_NARROW
    full_peer = (narrow_index + jax.random.randint(subkeys[3], (accelerator_roster,), 1, N_NARROW, dtype=jnp.int32)) % N_NARROW
    list_index = jnp.arange(list_total, dtype=jnp.int32)[None, :]
    counts = jnp.where(list_index == full_peer[:, None], HALO_CAP, counts)
    allowed = jnp.where(list_index < N_NARROW, list_index != narrow_index[:, None], jnp.where(list_index == N_NARROW, wide_index[:, None] > 0, wide_index[:, None] < N_WIDE - 1))
    candidate = jnp.arange(list_total * HALO_CAP, dtype=jnp.int32)
    lane_of = candidate // HALO_CAP
    position = candidate % HALO_CAP
    referenced = allowed[:, lane_of] & (position[None, :] < counts[:, lane_of])
    chosen = shuffled[:, :list_total * HALO_CAP].astype(jnp.int32)
    pointer = jnp.where(referenced, face_total + candidate[None, :], jnp.take_along_axis(inside, chosen, axis=1))
    result = jax.vmap(lambda base, targets, entries: base.at[targets].set(entries))(inside, chosen, pointer)
    return result.reshape(accelerator_roster, 4, ELEM_DEV).transpose(1, 0, 2).reshape(4, accelerator_roster * ELEM_DEV)


def fault_plan(key):
    accelerator_roster = N_WIDE * N_NARROW
    face_total = 4 * ELEM_DEV
    subkeys = jax.random.split(jax.random.fold_in(key, 5), 4)
    raw_count = jax.random.randint(subkeys[0], (accelerator_roster,), 1, FAULT_DEV + 1, dtype=jnp.int32)
    live_count = jnp.maximum(raw_count * raw_count // FAULT_DEV, 1)
    busiest = jax.random.randint(subkeys[1], (), 0, accelerator_roster, dtype=jnp.int32)
    live_count = jnp.where(jnp.arange(accelerator_roster, dtype=jnp.int32) == busiest, FAULT_DEV, live_count)
    shuffled = jax.vmap(lambda subkey: jax.random.permutation(subkey, face_total))(jax.random.split(subkeys[2], accelerator_roster))
    owners = jax.vmap(lambda subkey: jax.random.permutation(subkey, accelerator_roster))(jax.random.split(subkeys[3], accelerator_roster))
    slot_ids = jnp.arange(FAULT_DEV, dtype=jnp.int32)
    is_live = slot_ids[None, :] < live_count[:, None]
    faces_out = jnp.where(is_live, shuffled[:, :FAULT_DEV].astype(jnp.int32), -1)
    owners_out = jnp.where(is_live, owners[:, slot_ids // PAIR_CAP].astype(jnp.int32), -1)
    return (faces_out.reshape(-1), owners_out.reshape(-1))


def draw_rupture_side_index(key, part):
    return fault_plan(key)[0]


def draw_rupture_seat_partition(key, part):
    return fault_plan(key)[1]


def place_ends(drawn, own_key, least, largest):
    dims = drawn.shape
    index_at = [jax.random.randint(jax.random.fold_in(own_key, axis), (), 0, dims[axis]) for axis in range(len(dims))]
    drawn = drawn.at[tuple(index_at)].set(least)
    longest = dims.index(max(dims))
    index_at[longest] = (index_at[longest] + 1) % dims[longest]
    return drawn.at[tuple(index_at)].set(largest)


def block_levels(key, dims, cuts, least, largest):
    level = 1.0
    for dim, blocks in cuts:
        steps = jax.random.uniform(jax.random.fold_in(jax.random.fold_in(key, 6), dim), (blocks,), jnp.float32, least / len(cuts), largest / len(cuts))
        level = level * jnp.repeat(jnp.exp(steps), dims[dim] // blocks).reshape((-1,) + (1,) * (len(dims) - 1 - dim))
    return level


def scatter_about(stream_key, shape, scale, limit, cuts=(), kind=jnp.bfloat16):
    factor_of = block_levels(stream_key, shape, cuts, -0.22, 0.18) if cuts else 1.0
    drawn = jax.random.normal(stream_key, shape, jnp.float32) * scale * factor_of
    return jnp.minimum(jnp.maximum(drawn, -limit), limit).astype(kind)


def setup_inputs(seed: int = 0) -> dict:
    splits = jax.random.split(jax.random.key(seed), 23)
    return {
        "modal_unknowns": scatter_about(splits[0], (QUANTS * BASIS, ELEMS), 1.0, 6.0, ((1, 128),), jnp.float32),
        "timestep_metric_scaling": jnp.clip(0.15 + 0.29999998 * jax.random.uniform(splits[1], (3, ELEMS), jnp.float32) ** block_levels(splits[1], (3, ELEMS), ((1, 128),), -0.2, 0.2), 0.15, 0.45),
        "surface_measure_quotient": jnp.clip(0.5 + 1.0 * jax.random.uniform(splits[2], (4, ELEMS), jnp.float32) ** block_levels(splits[2], (4, ELEMS), ((1, 128),), -0.2, 0.2), 0.5, 1.5),
        "elastic_directional_derivs": scatter_about(splits[3], (3, QUANTS, QUANTS), QUANTS ** -0.5, 2.0, (), jnp.float32),
        "predictor_derivatives": scatter_about(splits[4], (3, BASIS, BASIS), BASIS ** -0.5, 1.25, (), jnp.float32),
        "interior_gradient_tables": scatter_about(splits[5], (3, BASIS, BASIS), BASIS ** -0.5, 1.25, (), jnp.float32),
        "interior_restriction": scatter_about(splits[6], (4, FACE_BASIS, BASIS), BASIS ** -0.5, 1.25, (), jnp.float32),
        "surface_raise_tables": scatter_about(splits[7], (4, BASIS, FACE_BASIS), FACE_BASIS ** -0.5, 2.0, (), jnp.float32),
        "riemann_numerical_tables": scatter_about(splits[8], (2, QUANTS, QUANTS), QUANTS ** -0.5, 2.0, (), jnp.float32),
        "boundary_polynomials_sampled": scatter_about(splits[9], (POINTS, FACE_BASIS), FACE_BASIS ** -0.5, 2.0, (), jnp.float32),
        "quadrature_gather_weights": scatter_about(splits[10], (POINTS, FACE_BASIS), POINTS ** -0.5, 1.5, (), jnp.float32),
        "thermal_diffusion_resolvent": draw_thermal_diffusion_resolvent(jax.random.fold_in(splits[22], 71), 0),
        "hydraulic_diffusion_resolvent": draw_hydraulic_diffusion_resolvent(jax.random.fold_in(splits[22], 71), 0),
        "thermal_field": scatter_about(splits[13], (DEPTH_SAMPLES, RUPTURE_SITES), 1.0, 6.0, ((1, 128),), jnp.float32),
        "fluid_load": scatter_about(splits[14], (DEPTH_SAMPLES, RUPTURE_SITES), 1.0, 6.0, ((1, 128),), jnp.float32),
        "earlier_sliding_speed": jnp.clip(jnp.exp(math.log(2.0) - 3.6888794 * jax.random.uniform(splits[15], (RUPTURE_SITES,), jnp.float32) ** block_levels(splits[15], (RUPTURE_SITES,), ((0, 128),), -0.2, 0.2)), 0.05, 2.0),
        "instant_sensitivity_a": jnp.clip(jnp.exp(math.log(1.0) - 1.609438 * jax.random.uniform(splits[16], (RUPTURE_SITES,), jnp.float32) ** block_levels(splits[16], (RUPTURE_SITES,), ((0, 128),), -0.2, 0.2)), 0.2, 1.0),
        "aging_memory_theta": jnp.clip(0.2 + 0.6 * jax.random.uniform(splits[17], (RUPTURE_SITES,), jnp.float32) ** block_levels(splits[17], (RUPTURE_SITES,), ((0, 128),), -0.2, 0.2), 0.2, 0.8),
        "outbound_ghost_indices": place_ends(jax.random.randint(splits[18], (LISTS, HALO_CAP * DEVICES), 0, 4 * ELEM_DEV), jax.random.fold_in(splits[18], 1), 0, (4 * ELEM_DEV) - 1).astype(jnp.int32),
        "boundary_entry_index": draw_boundary_entry_index(jax.random.fold_in(splits[22], 71), 0),
        "rupture_side_index": draw_rupture_side_index(jax.random.fold_in(splits[22], 71), 0),
        "rupture_seat_partition": draw_rupture_seat_partition(jax.random.fold_in(splits[22], 71), 0),
    }


largest_magnitude = lax.Precision.HIGHEST
shear_dissipation_warming = 0.5
thermal_multiplier = 0.5
background = 2.0
damping = 1.0

def inverse_sinh(value):
    magnitude = jnp.abs(value)
    return jnp.sign(value) * jnp.log(magnitude + jnp.sqrt(1.0 + magnitude * magnitude))

def element_section(modal_unknowns, timestep_metric_scaling, elastic_directional_derivs, predictor_derivatives, interior_gradient_tables, interior_restriction):
    unknown_kinds_total = elastic_directional_derivs.shape[1]
    basis_count = predictor_derivatives.shape[1]
    elem_count = modal_unknowns.shape[1]
    state_field = modal_unknowns.reshape(unknown_kinds_total, basis_count, elem_count)
    integral = state_field
    derivative = state_field
    factor = 1.0
    for degree in range(1, 4):
        starred = jnp.einsum('dqp,pbe->dqbe', elastic_directional_derivs, derivative, precision=largest_magnitude)
        derivative = -jnp.einsum('dbc,dqce,de->qbe', predictor_derivatives, starred, timestep_metric_scaling, precision=largest_magnitude)
        factor = factor * (degree + 1)
        integral = integral + derivative / factor
    starred = jnp.einsum('dqp,pbe->dqbe', elastic_directional_derivs, integral, precision=largest_magnitude)
    volume = jnp.einsum('dbc,dqce,de->qbe', interior_gradient_tables, starred, timestep_metric_scaling, precision=largest_magnitude)
    partial_value = (state_field + volume).reshape(unknown_kinds_total * basis_count, elem_count)
    boundary_polynomials = interior_restriction.shape[1]
    traces = jnp.einsum('fjb,qbe->qjfe', interior_restriction, integral, precision=largest_magnitude)
    return (partial_value, traces.reshape(unknown_kinds_total * boundary_polynomials, 4 * elem_count))

def fault_pack(traces, outside, rupture_side_index):
    face_count = traces.shape[1]
    column = jnp.clip(rupture_side_index, 0, face_count - 1)
    is_live = (rupture_side_index >= 0)[None, :]
    payload = jnp.concatenate([traces[:, column], outside[:, column]], axis=0)
    return jnp.where(is_live, payload, 0.0)

def to_owner(payload, rupture_seat_partition, pair_cap, accelerator_roster):
    row_count = payload.shape[0]
    blocked = payload.reshape(row_count, accelerator_roster, pair_cap).transpose(2, 0, 1)
    block_owner = rupture_seat_partition.reshape(accelerator_roster, pair_cap)[:, 0]
    destination = jnp.where(block_owner < 0, accelerator_roster, block_owner)
    buffer = jnp.zeros((pair_cap, row_count, accelerator_roster), payload.dtype)
    buffer = buffer.at[:, :, destination].set(blocked, mode='drop')
    return buffer.reshape(pair_cap * row_count, accelerator_roster)

def from_exchange(arrived, pair_cap):
    accelerator_roster = arrived.shape[1]
    row_count = arrived.shape[0] // pair_cap
    return arrived.reshape(pair_cap, row_count, accelerator_roster).transpose(1, 2, 0).reshape(row_count, accelerator_roster * pair_cap)

def to_return(prescribed_weight, pair_cap):
    row_count = prescribed_weight.shape[0]
    accelerator_roster = prescribed_weight.shape[1] // pair_cap
    return prescribed_weight.reshape(row_count, accelerator_roster, pair_cap).transpose(2, 0, 1).reshape(pair_cap * row_count, accelerator_roster)

def from_return(returned, rupture_seat_partition, pair_cap):
    accelerator_roster = returned.shape[1]
    row_count = returned.shape[0] // pair_cap
    blocked = returned.reshape(pair_cap, row_count, accelerator_roster)
    block_owner = rupture_seat_partition.reshape(accelerator_roster, pair_cap)[:, 0]
    picked = jnp.take(blocked, jnp.clip(block_owner, 0, accelerator_roster - 1), axis=2)
    return picked.transpose(1, 2, 0).reshape(row_count, accelerator_roster * pair_cap)

def sliding_resistance_rule(partition_extent, thermal_field, fluid_load, earlier_sliding_speed, instant_sensitivity_a, aging_memory_theta, boundary_polynomials_sampled, quadrature_gather_weights, thermal_diffusion_resolvent, hydraulic_diffusion_resolvent, unknown_kinds_total):
    seat_total = partition_extent.shape[1]
    points = boundary_polynomials_sampled.shape[0]
    boundary_polynomials = boundary_polynomials_sampled.shape[1]
    both_sides = partition_extent.reshape(2, unknown_kinds_total, boundary_polynomials, seat_total)
    values = jnp.einsum('gj,aqjs->aqsg', boundary_polynomials_sampled, both_sides, precision=largest_magnitude).reshape(2, unknown_kinds_total, seat_total * points)
    minus_side = values[0]
    plus_side = values[1]
    locked_shear = 0.5 * (minus_side[3] + plus_side[3]) + 0.5 * (plus_side[6] - minus_side[6])
    normal_stress = 0.5 * (minus_side[0] + plus_side[0]) + 0.5 * (plus_side[7] - minus_side[7])
    depth_sample_total = thermal_field.shape[0]
    node_depth = jnp.arange(depth_sample_total).astype(jnp.float32) / (depth_sample_total / 8.0)
    transverse_curve = jnp.exp(-node_depth * node_depth)
    warmed_curve = thermal_field + transverse_curve[:, None] * (shear_dissipation_warming * earlier_sliding_speed * earlier_sliding_speed)[None, :]
    refreshed_thermal_field = jnp.dot(thermal_diffusion_resolvent, warmed_curve, precision=largest_magnitude)
    refreshed_fluid_load = jnp.dot(hydraulic_diffusion_resolvent, fluid_load + thermal_multiplier * (refreshed_thermal_field - thermal_field), precision=largest_magnitude)
    effective = jax.nn.softplus(background + normal_stress - refreshed_fluid_load[0])
    weight = 0.5 * jnp.exp(aging_memory_theta / instant_sensitivity_a)
    sliding_speed = earlier_sliding_speed
    for newton_step in range(NEWTON):
        scaled = weight * sliding_speed
        mismatch = locked_shear - damping * sliding_speed - effective * instant_sensitivity_a * inverse_sinh(scaled)
        derivative = -damping - effective * instant_sensitivity_a * weight / jnp.sqrt(1.0 + scaled * scaled)
        sliding_speed = sliding_speed - mismatch / derivative
    traction = locked_shear - damping * sliding_speed
    middle = 0.5 * (minus_side + plus_side)
    quantity_row = jnp.arange(unknown_kinds_total)[:, None]
    imposed = jnp.where(quantity_row == 3, traction[None, :], jnp.where(quantity_row == 6, middle + 0.5 * sliding_speed[None, :], middle))
    prescribed_weight = jnp.einsum('qsg,gj->qjs', imposed.reshape(unknown_kinds_total, seat_total, points), quadrature_gather_weights, precision=largest_magnitude)
    return (prescribed_weight.reshape(unknown_kinds_total * boundary_polynomials, seat_total), refreshed_thermal_field, refreshed_fluid_load, sliding_speed)

def finish(partial_value, traces, outside, imposed, rupture_side_index, surface_measure_quotient, riemann_numerical_tables, surface_raise_tables):
    row_total, face_count = traces.shape
    basis_count = surface_raise_tables.shape[1]
    boundary_polynomials = surface_raise_tables.shape[2]
    unknown_kinds_total = row_total // boundary_polynomials
    elem_count = face_count // 4
    inside_trace = traces.reshape(unknown_kinds_total, boundary_polynomials, face_count)
    outside_trace = outside.reshape(unknown_kinds_total, boundary_polynomials, face_count)
    face_flux = jnp.einsum('qp,pjx->qjx', riemann_numerical_tables[0], inside_trace, precision=largest_magnitude)
    face_flux = face_flux + jnp.einsum('qp,pjx->qjx', riemann_numerical_tables[1], outside_trace, precision=largest_magnitude)
    fault_flux = jnp.einsum('qp,pjs->qjs', riemann_numerical_tables[0] + riemann_numerical_tables[1], imposed.reshape(unknown_kinds_total, boundary_polynomials, -1), precision=largest_magnitude)
    target = jnp.where(rupture_side_index < 0, face_count, rupture_side_index)
    face_flux = face_flux.at[:, :, target].set(fault_flux, mode='drop')
    surface = jnp.einsum('fbj,qjfe,fe->qbe', surface_raise_tables, face_flux.reshape(unknown_kinds_total, boundary_polynomials, 4, elem_count), surface_measure_quotient, precision=largest_magnitude)
    return partial_value - surface.reshape(unknown_kinds_total * basis_count, elem_count)

def divided_indices(array, column_width, accelerator_roster):
    return array.reshape(array.shape[0], accelerator_roster, column_width).transpose(1, 0, 2)

def merged_indices(array):
    return array.transpose(1, 0, 2).reshape(array.shape[1], array.shape[0] * array.shape[2])

def reference(modal_unknowns, timestep_metric_scaling, surface_measure_quotient, elastic_directional_derivs, predictor_derivatives, interior_gradient_tables, interior_restriction, surface_raise_tables, riemann_numerical_tables, boundary_polynomials_sampled, quadrature_gather_weights, thermal_diffusion_resolvent, hydraulic_diffusion_resolvent, thermal_field, fluid_load, earlier_sliding_speed, instant_sensitivity_a, aging_memory_theta, outbound_ghost_indices, boundary_entry_index, rupture_side_index, rupture_seat_partition):
    accelerator_roster = N_WIDE * N_NARROW
    unknown_kinds_total = QUANTS
    row_count = QUANTS * FACE_BASIS
    solution_part = divided_indices(modal_unknowns, ELEM_DEV, accelerator_roster)
    geometry_part = divided_indices(timestep_metric_scaling, ELEM_DEV, accelerator_roster)
    area_part = divided_indices(surface_measure_quotient, ELEM_DEV, accelerator_roster)
    send_part = divided_indices(outbound_ghost_indices, HALO_CAP, accelerator_roster)
    source_part = divided_indices(boundary_entry_index, ELEM_DEV, accelerator_roster).reshape(accelerator_roster, 4 * ELEM_DEV)
    face_part = rupture_side_index.reshape(accelerator_roster, FAULT_DEV)
    owner_part = rupture_seat_partition.reshape(accelerator_roster, FAULT_DEV)

    def section_one(operands):
        return element_section(operands[0], operands[1], elastic_directional_derivs, predictor_derivatives, interior_gradient_tables, interior_restriction)
    partial_all, traces_all = lax.map(section_one, (solution_part, geometry_part))

    def lists_of(traces, columns):
        taken = jnp.take(traces, columns.reshape(-1), axis=1)
        return taken.reshape(row_count, LISTS, HALO_CAP).transpose(1, 0, 2)
    sent = jax.vmap(lists_of)(traces_all, send_part)
    grid = sent.reshape(N_WIDE, N_NARROW, LISTS, row_count, HALO_CAP)
    narrow_in = grid[:, :, :N_NARROW].transpose(0, 2, 3, 1, 4).reshape(accelerator_roster, row_count, N_NARROW * HALO_CAP)
    upward = grid[:, :, N_NARROW]
    downward = grid[:, :, N_NARROW + 1]
    empty_row = jnp.zeros((1, N_NARROW, row_count, HALO_CAP), jnp.float32)
    from_lower = jnp.concatenate([empty_row, upward[:-1]], axis=0).reshape(accelerator_roster, row_count, HALO_CAP)
    from_upper = jnp.concatenate([downward[1:], empty_row], axis=0).reshape(accelerator_roster, row_count, HALO_CAP)
    received_all = jnp.concatenate([narrow_in, from_lower, from_upper], axis=2)

    def section_two(operands):
        traces, received, sources, faces = operands
        outside = jnp.take(jnp.concatenate([traces, received], axis=1), sources, axis=1)
        return fault_pack(traces, outside, faces)
    payload_all = lax.map(section_two, (traces_all, received_all, source_part, face_part))
    outgoing = jax.vmap(lambda payload, owners: to_owner(payload, owners, PAIR_CAP, accelerator_roster))(payload_all, owner_part)
    arrived = outgoing.transpose(2, 1, 0)
    partition_perspectives = jax.vmap(lambda block: from_exchange(block, PAIR_CAP))(arrived)
    sample_indices = FAULT_DEV * POINTS
    thermal_share = divided_indices(thermal_field, sample_indices, accelerator_roster)
    fluid_load_share = divided_indices(fluid_load, sample_indices, accelerator_roster)
    speed_share = earlier_sliding_speed.reshape(accelerator_roster, sample_indices)
    parameter_share = instant_sensitivity_a.reshape(accelerator_roster, sample_indices)
    memory_share = aging_memory_theta.reshape(accelerator_roster, sample_indices)

    def segment_third(operands):
        return sliding_resistance_rule(operands[0], operands[1], operands[2], operands[3], operands[4], operands[5], boundary_polynomials_sampled, quadrature_gather_weights, thermal_diffusion_resolvent, hydraulic_diffusion_resolvent, unknown_kinds_total)
    prescribed_everywhere, refreshed_thermal_field, refreshed_fluid_load, advanced_sliding_speed = lax.map(segment_third, (partition_perspectives, thermal_share, fluid_load_share, speed_share, parameter_share, memory_share))
    back_out = jax.vmap(lambda block: to_return(block, PAIR_CAP))(prescribed_everywhere)
    back_in = back_out.transpose(2, 1, 0)
    imposed_slots = jax.vmap(lambda block, owners: from_return(block, owners, PAIR_CAP))(back_in, owner_part)

    def section_four(operands):
        partial_value, traces, received, sources, faces, imposed, areas = operands
        outside = jnp.take(jnp.concatenate([traces, received], axis=1), sources, axis=1)
        return finish(partial_value, traces, outside, imposed, faces, areas, riemann_numerical_tables, surface_raise_tables)
    refreshed = lax.map(section_four, (partial_all, traces_all, received_all, source_part, face_part, imposed_slots, area_part))
    return (merged_indices(refreshed), merged_indices(refreshed_thermal_field), merged_indices(refreshed_fluid_load), advanced_sliding_speed.reshape(-1))
```

```python
import jax
import jax.numpy as jnp
import numpy as np
from jax import lax
from jax.experimental import pallas as pl
from jax.experimental.pallas import tpu as pltpu
from jax.sharding import PartitionSpec as P

NEWTON = 4
Q, NB, NJ, NG = 9, 20, 10, 16
LANES = 128
ROWS = Q * NB
HIGHEST = lax.Precision.HIGHEST
F32 = jnp.float32
BF16 = jnp.bfloat16
VMEM = pltpu.MemorySpace.VMEM
SMEM = pltpu.MemorySpace.SMEM
LIMIT = pltpu.CompilerParams(vmem_limit_bytes=56 * 1024 * 1024)


def tables():
    e = np.zeros((ROWS, Q), np.float32)
    f = np.zeros((ROWS, NB), np.float32)
    for q in range(Q):
        for b in range(NB):
            e[q * NB + b, q] = 1
            f[q * NB + b, b] = 1
    g = np.zeros((LANES, Q), np.float32)
    h = np.zeros((LANES, NJ), np.float32)
    for q in range(Q):
        for j in range(NJ):
            g[q * NJ + j, q] = 1
            h[q * NJ + j, j] = 1
    tile = np.zeros((LANES, NG), np.float32)
    for lane in range(LANES):
        tile[lane, lane % NG] = 1
    side = np.zeros((LANES, 4), np.float32)
    for q, column, low, high in ((3, 0, 0.5, 0.5), (6, 0, -0.5, 0.5), (0, 1, 0.5, 0.5), (7, 1, -0.5, 0.5)):
        side[q * NJ : (q + 1) * NJ, column] = low
        side[q * NJ : (q + 1) * NJ, 2 + column] = high
    mid = np.zeros((2, Q, Q), np.float32)
    mid[:] = 0.5 * np.eye(Q)
    mid[0, 6, 3] = -0.5
    mid[1, 6, 3] = 0.5
    linear = np.stack([g @ mid[0] @ g.T, g @ mid[1] @ g.T])
    slip = np.zeros((1, LANES), np.float32)
    slip[0, 3 * NJ : 4 * NJ] = -1.0
    slip[0, 6 * NJ : 7 * NJ] = 0.5
    pair = np.zeros((64, LANES), np.float32)
    for s in range(LANES):
        pair[s // 2, s] = 1
    return e, f, g, h, tile, side, linear, slip, pair


def dot(a, b, ca=1, cb=0, precision=HIGHEST):
    return lax.dot_general(
        a, b, (((ca,), (cb,)), ((), ())), precision=precision, preferred_element_type=F32
    )


def halves(x):
    high = x.astype(BF16)
    return high, (x - high.astype(F32)).astype(BF16)


def dot3(ah, al, bh, bl, cb=0):
    d = lambda a, b: lax.dot_general(
        a, b, (((1,), (cb,)), ((), ())), preferred_element_type=F32
    )
    return d(ah, bh) + (d(ah, bl) + d(al, bh))


def prepare_kernel(
    a, pd, kd, rs, sr, rt, bp, qg, cc, e, f, g, h, tile, side, linear, slip,
    mp_h, mp_l, mi_h, mi_l, wt_h, wt_l, wf_h, wf_l, ws_h, ws_l, wl, lin, vm,
):
    e_, f_, g_, h_ = e[...], f[...], g[...], h[...]

    def put(high, low, at, value):
        top, bottom = halves(value)
        high[at] = top
        low[at] = bottom

    for d in range(3):
        left = dot(dot(e_, a[d]), e_, 1, 1)
        put(mp_h, mp_l, d, -left * dot(dot(f_, pd[d]), f_, 1, 1))
        put(mi_h, mi_l, d, left * dot(dot(f_, kd[d]), f_, 1, 1))
    same = dot(e_, g_, 1, 1)
    r0 = dot(dot(e_, rt[0]), g_, 1, 1)
    r1 = dot(dot(e_, rt[1]), g_, 1, 1)
    for face in range(4):
        put(wt_h, wt_l, face, same * dot(dot(f_, rs[face], 1, 1), h_, 1, 1))
        lift = dot(dot(f_, sr[face]), h_, 1, 1)
        put(wf_h, wf_l, face, r0 * lift)
        put(wf_h, wf_l, 4 + face, r1 * lift)
        put(ws_h, ws_l, face, (r0 + r1) * lift)
    hb = dot(dot(h_, bp[...], 1, 1), tile[...], 1, 1)
    for i in range(4):
        wl[i] = hb * side[:, i : i + 1]
    hch = dot(dot(h_, cc[...]), h_, 1, 1)
    lin[0] = hch * linear[0]
    lin[1] = hch * linear[1]
    vm[...] = dot(dot(tile[...], qg[...]), h_, 1, 1) * slip[...]


def predictor_kernel(u, t, mp_h, mp_l, wt_h, wt_l, integral, faces, padded):
    times = t[...]
    current = u[...]
    total = current
    factor = 1.0
    for degree in range(1, 4):
        xh, xl = halves(current)
        current = (
            dot3(mp_h[0], mp_l[0], xh, xl) * times[0:1]
            + dot3(mp_h[1], mp_l[1], xh, xl) * times[1:2]
            + dot3(mp_h[2], mp_l[2], xh, xl) * times[2:3]
        )
        factor = factor * (degree + 1)
        total = total + current * (1.0 / factor)
    integral[...] = total
    padded[...] = jnp.zeros(padded.shape, F32)
    padded[0:ROWS, :] = total
    turned = padded[...].T[:, 0:ROWS]
    xh, xl = halves(turned)
    for face in range(4):
        faces[face] = dot3(xh, xl, wt_h[face], wt_l[face])


def volume_kernel(u, t, integral, mi_h, mi_l, partial):
    times = t[...]
    xh, xl = halves(integral[...])
    partial[...] = (
        u[...]
        + dot3(mi_h[0], mi_l[0], xh, xl) * times[0:1]
        + dot3(mi_h[1], mi_l[1], xh, xl) * times[1:2]
        + dot3(mi_h[2], mi_l[2], xh, xl) * times[2:3]
    )


def send_kernel(index, faces, group, lower, upper):
    for r in range(6):
        target, base = (group, r * 512) if r < 4 else ((lower, 0) if r == 4 else (upper, 0))

        def body(i, carry, r=r, target=target, base=base):
            for k in range(16):
                n = i * 16 + k
                target[pl.ds(base + n, 1), :] = faces[pl.ds(index[r, n], 1), :]
            return carry

        lax.fori_loop(0, 32, body, 0)


def thermal_kernel(th, fl, speed, shape, tr, hr, new_th, new_fl, top):
    v = speed[...]
    old = th[...]
    warmed = old + shape[...] * (0.5 * v * v)
    ah, al = halves(tr[...])
    xh, xl = halves(warmed)
    fresh = dot3(ah, al, xh, xl)
    new_th[...] = fresh
    bh, bl = halves(hr[...])
    yh, yl = halves(fl[...] + 0.5 * (fresh - old))
    pressure = dot3(bh, bl, yh, yl)
    new_fl[...] = pressure
    for r in range(top.shape[0]):
        top[r : r + 1, :] = pressure[0:1, r * LANES : (r + 1) * LANES]


def payload_kernel(slot, entry, faces, group, lower, upper, payload, table):
    count = faces.shape[0]
    extent = count + group.shape[0] + lower.shape[0] + upper.shape[0]
    table[0:count, :] = faces[...]
    at = count
    for part in (group, lower, upper):
        table[at : at + part.shape[0], :] = part[...]
        at += part.shape[0]
    table[extent : extent + 8, :] = jnp.zeros((8, LANES), F32)

    def body(o, carry):
        for k in range(4):
            face = slot[o, k]
            live = face >= 0
            safe = jnp.maximum(face, 0)
            inner = jnp.where(live, face, extent)
            outer = jnp.where(live, entry[lax.shift_right_logical(safe, 11), safe & 2047], extent)
            payload[pl.ds(o * 8 + k, 1), :] = table[pl.ds(inner, 1), :]
            payload[pl.ds(o * 8 + 4 + k, 1), :] = table[pl.ds(outer, 1), :]
        return carry

    lax.fori_loop(0, slot.shape[0], body, 0)


def outside_kernel(
    entry, faces, group, lower, upper, partial, area, wf_h, wf_l, base, table, outside
):
    count = faces.shape[0]
    table[0:count, :] = faces[...]
    at = count
    for part in (group, lower, upper):
        table[at : at + part.shape[0], :] = part[...]
        at += part.shape[0]
    elems = count // 4
    result = partial[...]
    for face in range(4):

        def body(i, carry, face=face):
            for k in range(16):
                n = i * 16 + k
                outside[pl.ds(n, 1), :] = table[pl.ds(entry[face, n], 1), :]
            return carry

        lax.fori_loop(0, elems // 16, body, 0)
        th, tl = halves(table[face * elems : (face + 1) * elems, :])
        oh, ol = halves(outside[...])
        flux = dot3(wf_h[face], wf_l[face], th, tl, 1) + dot3(
            wf_h[4 + face], wf_l[4 + face], oh, ol, 1
        )
        result = result - flux * area[face : face + 1, :]
    base[...] = result


def fault_kernel(arrived, top, speed, sense, memory, wl, lin, vm, pair, imposed, rate):
    lanes = lax.shift_right_logical(lax.broadcasted_iota(jnp.int32, (LANES, LANES), 1), 4)
    half = (lax.broadcasted_iota(jnp.int32, (LANES, LANES), 0) & 1) * 4
    locked = jnp.zeros((LANES, LANES), F32)
    normal = jnp.zeros((LANES, LANES), F32)
    for k in range(4):
        minus = arrived[pl.ds(k, LANES, stride=8), :]
        plus = arrived[pl.ds(4 + k, LANES, stride=8), :]
        mine = lanes == half + k
        locked = locked + jnp.where(mine, dot(minus, wl[0]) + dot(plus, wl[2]), 0.0)
        normal = normal + jnp.where(mine, dot(minus, wl[1]) + dot(plus, wl[3]), 0.0)
    locked = dot(pair[...], locked)
    normal = dot(pair[...], normal)
    excess = 2.0 + normal - top[...]
    effective = jnp.maximum(excess, 0.0) + jnp.log1p(jnp.exp(-jnp.abs(excess)))
    strength = effective * sense[...]
    weight = 0.5 * jnp.exp(memory[...] / sense[...])
    v = speed[...]
    for _ in range(NEWTON):
        scaled = weight * v
        root = jnp.sqrt(1.0 + scaled * scaled)
        size = jnp.log(jnp.abs(scaled) + root)
        mismatch = locked - v - strength * jnp.where(scaled < 0.0, -size, size)
        slope = -1.0 - strength * weight / root
        v = v - mismatch / slope
    rate[...] = v
    spread = dot(pair[...], v, 0, 0)
    for k in range(4):
        minus = arrived[pl.ds(k, LANES, stride=8), :]
        plus = arrived[pl.ds(4 + k, LANES, stride=8), :]
        mine = jnp.where(lanes == half + k, spread, 0.0)
        imposed[pl.ds(k, LANES, stride=4), :] = (
            dot(minus, lin[0]) + dot(plus, lin[1]) + dot(mine, vm[...])
        )


def finish_kernel(slot, returned, base, area, ws_h, ws_l, out, spread):
    count = spread.shape[0] - 8
    elems = count // 4
    spread[...] = jnp.zeros(spread.shape, F32)

    def body(o, carry):
        for k in range(4):
            face = slot[o, k]
            target = jnp.where(face >= 0, face, count)
            spread[pl.ds(target, 1), :] = returned[pl.ds(o * 4 + k, 1), :]
        return carry

    lax.fori_loop(0, slot.shape[0], body, 0)
    result = base[...]
    for face in range(4):
        zh, zl = halves(spread[face * elems : (face + 1) * elems, :])
        result = result - dot3(ws_h[face], ws_l[face], zh, zl, 1) * area[face : face + 1, :]
    out[...] = result


def shaped(shape, dtype=F32):
    return jax.ShapeDtypeStruct(shape, dtype)


def whole(count, smem=()):
    return [pl.BlockSpec(memory_space=SMEM if i in smem else VMEM) for i in range(count)]


def shift(array, axis, by):
    peers = lax.axis_size(axis)
    pairs = [(i, i + by) for i in range(peers) if 0 <= i + by < peers]
    return lax.ppermute(array, axis, pairs)


def per_device(
    modal_unknowns,
    timestep_metric_scaling,
    surface_measure_quotient,
    elastic_directional_derivs,
    predictor_derivatives,
    interior_gradient_tables,
    interior_restriction,
    surface_raise_tables,
    riemann_numerical_tables,
    boundary_polynomials_sampled,
    quadrature_gather_weights,
    thermal_diffusion_resolvent,
    hydraulic_diffusion_resolvent,
    thermal_field,
    fluid_load,
    earlier_sliding_speed,
    instant_sensitivity_a,
    aging_memory_theta,
    outbound_ghost_indices,
    boundary_entry_index,
    rupture_side_index,
    rupture_seat_partition,
):
    elems = modal_unknowns.shape[1]
    faces_total = 4 * elems
    devices = lax.axis_size(("wide", "narrow"))
    points = thermal_field.shape[1]
    e, f, g, h, tile, side, linear, slip, pair = tables()
    cross = lax.dot_general(
        boundary_polynomials_sampled,
        quadrature_gather_weights,
        (((0,), (0,)), ((), ())),
        precision=HIGHEST,
    )

    owners = rupture_seat_partition.reshape(devices, 4)[:, 0]
    listed = (owners[None, :] == jnp.arange(devices, dtype=jnp.int32)[:, None])[:, :, None]
    slot = jnp.sum(jnp.where(listed, rupture_side_index.reshape(devices, 4)[None] + 1, 0), axis=1) - 1
    ruptured = jnp.any(
        rupture_side_index[:, None, None]
        == jnp.arange(faces_total, dtype=jnp.int32).reshape(1, 4, elems),
        axis=0,
    )
    open_area = jnp.where(ruptured, 0.0, surface_measure_quotient)

    wide = (ROWS, LANES)
    (mp_h, mp_l, mi_h, mi_l, wt_h, wt_l, wf_h, wf_l, ws_h, ws_l, wl, lin, vm) = pl.pallas_call(
        prepare_kernel,
        in_specs=whole(17),
        out_specs=whole(13),
        out_shape=[shaped((3, ROWS, ROWS), BF16)] * 4
        + [shaped((4,) + wide, BF16)] * 2
        + [shaped((8,) + wide, BF16)] * 2
        + [shaped((4,) + wide, BF16)] * 2
        + [shaped((4, LANES, LANES)), shaped((2, LANES, LANES)), shaped((LANES, LANES))],
        compiler_params=LIMIT,
        name="prepare",
    )(
        elastic_directional_derivs,
        predictor_derivatives,
        interior_gradient_tables,
        interior_restriction,
        surface_raise_tables,
        riemann_numerical_tables,
        boundary_polynomials_sampled,
        quadrature_gather_weights,
        cross,
        e, f, g, h, tile, side, linear, slip,
    )

    step = 512
    column = lambda rows: pl.BlockSpec((rows, step), lambda i: (0, i))
    fixed = lambda shape: pl.BlockSpec(shape, lambda i: (0,) * len(shape))
    square = fixed((3, ROWS, ROWS))
    integral, face_rows = pl.pallas_call(
        predictor_kernel,
        grid=(elems // step,),
        in_specs=[column(ROWS), column(3), square, square, fixed((4,) + wide), fixed((4,) + wide)],
        out_specs=[column(ROWS), pl.BlockSpec((4, step, LANES), lambda i: (0, i, 0))],
        out_shape=[shaped((ROWS, elems)), shaped((4, elems, LANES))],
        scratch_shapes=[pltpu.VMEM((256, step), F32)],
        compiler_params=LIMIT,
        name="predictor",
    )(modal_unknowns, timestep_metric_scaling, mp_h, mp_l, wt_h, wt_l)
    face_rows = face_rows.reshape(faces_total, LANES)

    group_out, lower_out, upper_out = pl.pallas_call(
        send_kernel,
        in_specs=whole(2, (0,)),
        out_specs=whole(3),
        out_shape=[shaped((2048, LANES)), shaped((512, LANES)), shaped((512, LANES))],
        compiler_params=LIMIT,
        name="halo_rows",
    )(outbound_ghost_indices, face_rows)
    group = lax.all_to_all(group_out, "narrow", split_axis=0, concat_axis=0, tiled=True)
    lower = shift(lower_out, "wide", 1)
    upper = shift(upper_out, "wide", -1)

    width = 1024
    block = pl.BlockSpec((64, width), lambda i: (0, i))
    depth = jnp.arange(64).astype(F32) / 8.0
    curve = jnp.exp(-depth * depth)[:, None]
    new_temperature, new_pressure, top = pl.pallas_call(
        thermal_kernel,
        grid=(points // width,),
        in_specs=[
            block, block, pl.BlockSpec((1, width), lambda i: (0, i)),
            fixed((64, 1)), fixed((64, 64)), fixed((64, 64)),
        ],
        out_specs=[block, block, pl.BlockSpec((width // LANES, LANES), lambda i: (i, 0))],
        out_shape=[shaped((64, points)), shaped((64, points)), shaped((points // LANES, LANES))],
        compiler_params=LIMIT,
        name="thermal",
    )(
        thermal_field, fluid_load, earlier_sliding_speed.reshape(1, points), curve,
        thermal_diffusion_resolvent, hydraulic_diffusion_resolvent,
    )

    partial = pl.pallas_call(
        volume_kernel,
        grid=(elems // step,),
        in_specs=[column(ROWS), column(3), column(ROWS), square, square],
        out_specs=column(ROWS),
        out_shape=shaped((ROWS, elems)),
        compiler_params=LIMIT,
        name="volume",
    )(modal_unknowns, timestep_metric_scaling, integral, mi_h, mi_l)

    extent = faces_total + 3072
    payload = pl.pallas_call(
        payload_kernel,
        in_specs=whole(6, (0, 1)),
        out_specs=whole(1)[0],
        out_shape=shaped((devices * 8, LANES)),
        scratch_shapes=[pltpu.VMEM((extent + 8, LANES), F32)],
        compiler_params=LIMIT,
        name="payload",
    )(slot, boundary_entry_index, face_rows, group, lower, upper)
    arrived = lax.all_to_all(payload, ("wide", "narrow"), split_axis=0, concat_axis=0, tiled=True)

    base = pl.pallas_call(
        outside_kernel,
        in_specs=whole(9, (0,)),
        out_specs=whole(1)[0],
        out_shape=shaped((ROWS, elems)),
        scratch_shapes=[pltpu.VMEM((extent, LANES), F32), pltpu.VMEM((elems, LANES), F32)],
        compiler_params=LIMIT,
        name="outside",
    )(boundary_entry_index, face_rows, group, lower, upper, partial, open_area, wf_h, wf_l)

    flat = lambda x: x.reshape(points // LANES, LANES)
    imposed, rate = pl.pallas_call(
        fault_kernel,
        in_specs=whole(9),
        out_specs=whole(2),
        out_shape=[shaped((devices * 4, LANES)), shaped((points // LANES, LANES))],
        compiler_params=LIMIT,
        name="fault",
    )(
        arrived, top, flat(earlier_sliding_speed), flat(instant_sensitivity_a),
        flat(aging_memory_theta), wl, lin, vm, pair,
    )
    returned = lax.all_to_all(imposed, ("wide", "narrow"), split_axis=0, concat_axis=0, tiled=True)

    advanced = pl.pallas_call(
        finish_kernel,
        in_specs=whole(6, (0,)),
        out_specs=whole(1)[0],
        out_shape=shaped((ROWS, elems)),
        scratch_shapes=[pltpu.VMEM((faces_total + 8, LANES), F32)],
        compiler_params=LIMIT,
        name="finish",
    )(slot, returned, base, surface_measure_quotient, ws_h, ws_l)
    return advanced, new_temperature, new_pressure, rate.reshape(points)


def solution(mesh):
    split = P(None, ("wide", "narrow"))
    flat = P(("wide", "narrow"))
    return jax.shard_map(
        per_device,
        mesh=mesh,
        in_specs=(split,) * 3 + (P(),) * 10 + (split,) * 2 + (flat,) * 3 + (split,) * 2 + (flat,) * 2,
        out_specs=(split, split, split, flat),
        check_vma=False,
    )
```

```python
import jax
import jax.numpy as jnp
import numpy as np
from jax import lax
from jax.experimental import pallas as pl
from jax.experimental.pallas import tpu as pltpu
from jax.sharding import PartitionSpec as P

NEWTON = 4
Q, NB, NJ, NG = 9, 20, 10, 16
LANES = 128
ROWS = Q * NB
PAD = 192
HIGHEST = lax.Precision.HIGHEST
F32 = jnp.float32
BF16 = jnp.bfloat16
VMEM = pltpu.MemorySpace.VMEM
SMEM = pltpu.MemorySpace.SMEM
LIMIT = pltpu.CompilerParams(vmem_limit_bytes=56 * 1024 * 1024)


def tables():
    e = np.zeros((ROWS, Q), np.float32)
    f = np.zeros((ROWS, NB), np.float32)
    for q in range(Q):
        for b in range(NB):
            e[q * NB + b, q] = 1
            f[q * NB + b, b] = 1
    g = np.zeros((LANES, Q), np.float32)
    h = np.zeros((LANES, NJ), np.float32)
    for q in range(Q):
        for j in range(NJ):
            g[q * NJ + j, q] = 1
            h[q * NJ + j, j] = 1
    tile = np.zeros((LANES, NG), np.float32)
    for lane in range(LANES):
        tile[lane, lane % NG] = 1
    side = np.zeros((LANES, 4), np.float32)
    for q, column, low, high in ((3, 0, 0.5, 0.5), (6, 0, -0.5, 0.5), (0, 1, 0.5, 0.5), (7, 1, -0.5, 0.5)):
        side[q * NJ : (q + 1) * NJ, column] = low
        side[q * NJ : (q + 1) * NJ, 2 + column] = high
    mid = np.zeros((2, Q, Q), np.float32)
    mid[:] = 0.5 * np.eye(Q)
    mid[0, 6, 3] = -0.5
    mid[1, 6, 3] = 0.5
    linear = np.stack([g @ mid[0] @ g.T, g @ mid[1] @ g.T])
    slip = np.zeros((1, LANES), np.float32)
    slip[0, 3 * NJ : 4 * NJ] = -1.0
    slip[0, 6 * NJ : 7 * NJ] = 0.5
    pair = np.zeros((64, LANES), np.float32)
    for s in range(LANES):
        pair[s // 2, s] = 1
    return e, f, g, h, tile, side, linear, slip, pair


def dot(a, b, ca=1, cb=0, precision=HIGHEST):
    return lax.dot_general(
        a, b, (((ca,), (cb,)), ((), ())), precision=precision, preferred_element_type=F32
    )


def halves(x):
    high = x.astype(BF16)
    return high, (x - high.astype(F32)).astype(BF16)


def single(a, b, cb=0):
    return lax.dot_general(a, b, (((1,), (cb,)), ((), ())), preferred_element_type=F32)


def put(out, at, value, half):
    high, low = halves(value)
    rows, lanes = value.shape
    out[at[0] + (slice(at[1], at[1] + rows), slice(at[2], at[2] + lanes))] = high
    out[at[0] + (slice(half + at[1], half + at[1] + rows), slice(at[2], at[2] + lanes))] = low


def stacked(weights, x, cb=0):
    xh, xl = halves(x)
    half = weights.shape[0] // 2
    both = single(weights, xh, cb)
    return both[0:half] + (both[half:] + single(weights[0:half], xl, cb))


def prepare_kernel(a, pd, rs, e, f, g, h, mp, wt):
    e_, f_, g_, h_ = e[...], f[...], g[...], h[...]
    mp[...] = jnp.zeros(mp.shape, BF16)
    for d in range(3):
        left = dot(dot(e_, a[:, d, :]), e_, 1, 1)
        put(mp, ((), d * PAD, 0), -left * dot(dot(f_, pd[d]), f_, 1, 1), 3 * PAD)
    same = dot(e_, g_, 1, 1)
    for face in range(4):
        high, low = halves(same * dot(dot(f_, rs[:, face, :], 1, 1), h_, 1, 1))
        wt[0, :, face * LANES : (face + 1) * LANES] = high
        wt[1, :, face * LANES : (face + 1) * LANES] = low


def prepare_rest_kernel(
    a, kd, sr, rt, bp, qg, e, f, g, h, tile, side, linear, slip, mi, wf, ws, wm, wp, vm
):
    e_, f_, g_, h_ = e[...], f[...], g[...], h[...]
    mi[...] = jnp.zeros(mi.shape, BF16)
    wf[...] = jnp.zeros(wf.shape, BF16)
    ws[...] = jnp.zeros(ws.shape, BF16)
    for d in range(3):
        left = dot(dot(e_, a[:, d, :]), e_, 1, 1)
        put(mi, ((), d * PAD, 0), left * dot(dot(f_, kd[d]), f_, 1, 1), 3 * PAD)
    r0 = dot(dot(e_, rt[:, 0, :]), g_, 1, 1)
    r1 = dot(dot(e_, rt[:, 1, :]), g_, 1, 1)
    for face in range(4):
        lift = dot(dot(f_, sr[:, face, :], 1, 1), h_, 1, 1)
        put(wf, ((face,), 0, 0), r0 * lift, PAD)
        put(wf, ((face,), 0, LANES), r1 * lift, PAD)
        put(ws, ((face,), 0, 0), (r0 + r1) * lift, PAD)
    hb = dot(dot(h_, bp[...], 1, 1), tile[...], 1, 1)
    hch = dot(dot(h_, dot(bp[...], qg[...], 0, 0)), h_, 1, 1)
    for out, at in ((wm, 0), (wp, 1)):
        out[:, 0:LANES] = hb * side[:, 2 * at : 2 * at + 1]
        out[:, LANES : 2 * LANES] = hb * side[:, 2 * at + 1 : 2 * at + 2]
        out[:, 2 * LANES :] = hch * linear[at]
    vm[...] = dot(dot(tile[...], qg[...]), h_, 1, 1) * slip[...]


def directional(weights, x, times):
    y = stacked(weights, x)
    return (
        y[0:ROWS] * times[0:1]
        + y[PAD : PAD + ROWS] * times[1:2]
        + y[2 * PAD : 2 * PAD + ROWS] * times[2:3]
    )


def predictor_kernel(u, t, mp, wt, integral, faces, padded):
    times = t[...]
    current = u[...]
    total = current
    factor = 1.0
    for degree in range(1, 4):
        current = directional(mp[...], current, times)
        factor = factor * (degree + 1)
        total = total + current * (1.0 / factor)
    integral[...] = total
    padded[...] = jnp.zeros(padded.shape, F32)
    padded[0:ROWS, :] = total
    xh, xl = halves(padded[...].T[:, 0:ROWS])
    rows = single(xh, wt[0]) + (single(xh, wt[1]) + single(xl, wt[0]))
    for face in range(4):
        faces[face] = rows[:, face * LANES : (face + 1) * LANES]


def volume_kernel(u, t, integral, mi, partial):
    partial[...] = u[...] + directional(mi[...], integral[...], t[...])


def take_rows(index, start, count, source, target, base):
    def body(i, carry):
        first = i * 16
        rows = [source[pl.ds(index[start + first + k], 1), :] for k in range(16)]
        for k in range(16):
            target[pl.ds(base + first + k, 1), :] = rows[k]
        return carry

    lax.fori_loop(0, count // 16, body, 0)


def send_kernel(index, faces, group, lower, upper):
    take_rows(index, 0, 2048, faces, group, 0)
    take_rows(index, 2048, 512, faces, lower, 0)
    take_rows(index, 2560, 512, faces, upper, 0)


def thermal_kernel(th, fl, speed, shape, tr, hr, new_th, new_fl, top):
    v = speed[...]
    old = th[...]
    warmed = old + shape[...] * (0.5 * v * v)
    fresh = stacked(jnp.concatenate(halves(tr[...]), axis=0), warmed)
    new_th[...] = fresh
    pressure = stacked(jnp.concatenate(halves(hr[...]), axis=0), fl[...] + 0.5 * (fresh - old))
    new_fl[...] = pressure
    for r in range(top.shape[0]):
        top[r : r + 1, :] = pressure[0:1, r * LANES : (r + 1) * LANES]


def fill(table, parts, sems):
    at = 0
    copies = []
    for i, part in enumerate(parts):
        rows = part.shape[0]
        copies.append(pltpu.make_async_copy(part, table.at[pl.ds(at, rows)], sems.at[i]))
        at += rows
    for copy in copies:
        copy.start()
    for copy in copies:
        copy.wait()


def live_blocks(seat):
    return lax.fori_loop(
        0, seat.shape[0] // 4, lambda i, c: c + (seat[i * 4] >= 0).astype(jnp.int32), 0
    )


def payload_kernel(face, seat, entry, faces, group, lower, upper, payload, table, sems):
    extent = table.shape[0] - 8
    payload[...] = jnp.zeros(payload.shape, F32)
    table[extent : extent + 8, :] = jnp.zeros((8, LANES), F32)
    blocks = live_blocks(seat)
    fill(table, (faces, group, lower, upper), sems)

    def body(i, carry):
        owner = seat[i * 4]
        rows = []
        for k in range(4):
            column = face[i * 4 + k]
            live = column >= 0
            rows.append(table[pl.ds(jnp.where(live, column, extent), 1), :])
            outer = jnp.where(live, entry[jnp.maximum(column, 0)], extent)
            rows.append(table[pl.ds(outer, 1), :])
        for k in range(4):
            payload[pl.ds(owner * 8 + k, 1), :] = rows[2 * k]
            payload[pl.ds(owner * 8 + 4 + k, 1), :] = rows[2 * k + 1]
        return carry

    lax.fori_loop(0, blocks, body, 0)


def outside_kernel(first, entry, faces, group, lower, upper, partial, area, wf, base, table, outside, sems):
    fill(table, (faces, group, lower, upper), sems)
    elems = faces.shape[0] // 4
    result = partial[...]
    for face in (first, first + 1):
        take_rows(entry, face * elems, elems, table, outside, 0)
        rows = jnp.concatenate([table[face * elems : (face + 1) * elems, :], outside[...]], axis=1)
        flux = stacked(wf[face], rows, 1)
        result = result - flux[0:ROWS] * area[face : face + 1, :]
    base[...] = result


def fault_kernel(arrived, top, speed, sense, memory, wm, wp, vm, pair, imposed, rate):
    lanes = lax.shift_right_logical(lax.broadcasted_iota(jnp.int32, (LANES, LANES), 1), 4)
    half = (lax.broadcasted_iota(jnp.int32, (LANES, LANES), 0) & 1) * 4
    pick = lambda at: jnp.concatenate(
        [arrived[pl.ds(at + k, LANES, stride=8), :] for k in range(4)], axis=0
    )
    linear = dot(pick(0), wm[...]) + dot(pick(4), wp[...])
    locked = jnp.zeros((LANES, LANES), F32)
    normal = jnp.zeros((LANES, LANES), F32)
    for k in range(4):
        mine = lanes == half + k
        part = linear[k * LANES : (k + 1) * LANES]
        locked = locked + jnp.where(mine, part[:, 0:LANES], 0.0)
        normal = normal + jnp.where(mine, part[:, LANES : 2 * LANES], 0.0)
    locked = dot(pair[...], locked)
    normal = dot(pair[...], normal)
    excess = 2.0 + normal - top[...]
    effective = jnp.maximum(excess, 0.0) + jnp.log1p(jnp.exp(-jnp.abs(excess)))
    strength = effective * sense[...]
    weight = 0.5 * jnp.exp(memory[...] / sense[...])
    v = speed[...]
    for _ in range(NEWTON):
        scaled = weight * v
        root = jnp.sqrt(1.0 + scaled * scaled)
        size = jnp.log(jnp.abs(scaled) + root)
        mismatch = locked - v - strength * jnp.where(scaled < 0.0, -size, size)
        slope = -1.0 - strength * weight / root
        v = v - mismatch / slope
    rate[...] = v
    spread = dot(pair[...], v, 0, 0)
    mine = jnp.concatenate(
        [jnp.where(lanes == half + k, spread, 0.0) for k in range(4)], axis=0
    )
    result = linear[:, 2 * LANES :] + dot(mine, vm[...])
    for k in range(4):
        imposed[pl.ds(k, LANES, stride=4), :] = result[k * LANES : (k + 1) * LANES]


def finish_kernel(face, seat, returned, base, area, ws, out, spread, held, sems):
    copy = pltpu.make_async_copy(base, held, sems.at[0])
    copy.start()
    count = spread.shape[0] - 8
    elems = count // 4
    spread[...] = jnp.zeros(spread.shape, F32)

    def body(i, carry):
        owner = seat[i * 4]
        rows = [returned[pl.ds(owner * 4 + k, 1), :] for k in range(4)]
        for k in range(4):
            column = face[i * 4 + k]
            spread[pl.ds(jnp.where(column >= 0, column, count), 1), :] = rows[k]
        return carry

    lax.fori_loop(0, live_blocks(seat), body, 0)
    copy.wait()
    result = held[...]
    for at in range(4):
        flux = stacked(ws[at], spread[at * elems : (at + 1) * elems, :], 1)
        result = result - flux[0:ROWS] * area[at : at + 1, :]
    out[...] = result


def shaped(shape, dtype=F32):
    return jax.ShapeDtypeStruct(shape, dtype)


def whole(count, smem=(), left=()):
    space = lambda i: SMEM if i in smem else pl.ANY if i in left else VMEM
    return [pl.BlockSpec(memory_space=space(i)) for i in range(count)]


def shift(array, axis, by):
    peers = lax.axis_size(axis)
    pairs = [(i, i + by) for i in range(peers) if 0 <= i + by < peers]
    return lax.ppermute(array, axis, pairs)


def per_device(
    modal_unknowns,
    timestep_metric_scaling,
    surface_measure_quotient,
    elastic_directional_derivs,
    predictor_derivatives,
    interior_gradient_tables,
    interior_restriction,
    surface_raise_tables,
    riemann_numerical_tables,
    boundary_polynomials_sampled,
    quadrature_gather_weights,
    thermal_diffusion_resolvent,
    hydraulic_diffusion_resolvent,
    thermal_field,
    fluid_load,
    earlier_sliding_speed,
    instant_sensitivity_a,
    aging_memory_theta,
    outbound_ghost_indices,
    boundary_entry_index,
    rupture_side_index,
    rupture_seat_partition,
):
    elems = modal_unknowns.shape[1]
    faces_total = 4 * elems
    devices = lax.axis_size(("wide", "narrow"))
    points = thermal_field.shape[1]
    e, f, g, h, tile, side, linear, slip, pair = tables()
    ruptured = jnp.any(
        rupture_side_index[:, None, None]
        == jnp.arange(faces_total, dtype=jnp.int32).reshape(1, 4, elems),
        axis=0,
    )
    open_area = jnp.where(ruptured, 0.0, surface_measure_quotient)
    entry = boundary_entry_index.reshape(-1)
    elastic = jnp.transpose(elastic_directional_derivs, (1, 0, 2))

    mp, wt = pl.pallas_call(
        prepare_kernel,
        in_specs=whole(7),
        out_specs=whole(2),
        out_shape=[shaped((6 * PAD, ROWS), BF16), shaped((2, ROWS, 4 * LANES), BF16)],
        compiler_params=LIMIT,
        name="prepare",
    )(
        elastic, predictor_derivatives, jnp.transpose(interior_restriction, (1, 0, 2)), e, f, g, h
    )

    step = 512
    column = lambda rows: pl.BlockSpec((rows, step), lambda i: (0, i))
    fixed = lambda shape: pl.BlockSpec(shape, lambda i: (0,) * len(shape))
    integral, face_rows = pl.pallas_call(
        predictor_kernel,
        grid=(elems // step,),
        in_specs=[column(ROWS), column(3), fixed((6 * PAD, ROWS)), fixed((2, ROWS, 4 * LANES))],
        out_specs=[column(ROWS), pl.BlockSpec((4, step, LANES), lambda i: (0, i, 0))],
        out_shape=[shaped((ROWS, elems)), shaped((4, elems, LANES))],
        scratch_shapes=[pltpu.VMEM((256, step), F32)],
        compiler_params=LIMIT,
        name="predictor",
    )(modal_unknowns, timestep_metric_scaling, mp, wt)
    face_rows = face_rows.reshape(faces_total, LANES)

    group_out, lower_out, upper_out = pl.pallas_call(
        send_kernel,
        in_specs=whole(2, (0,)),
        out_specs=whole(3),
        out_shape=[shaped((2048, LANES)), shaped((512, LANES)), shaped((512, LANES))],
        compiler_params=LIMIT,
        name="halo_rows",
    )(outbound_ghost_indices.reshape(-1), face_rows)
    group = lax.all_to_all(group_out, "narrow", split_axis=0, concat_axis=0, tiled=True)
    lower = shift(lower_out, "wide", 1)
    upper = shift(upper_out, "wide", -1)

    tensors, sensitivity, _ = lax.optimization_barrier(
        (riemann_numerical_tables, thermal_diffusion_resolvent, lower_out)
    )
    mi, wf, ws, wm, wp, vm = pl.pallas_call(
        prepare_rest_kernel,
        in_specs=whole(14),
        out_specs=whole(6),
        out_shape=[
            shaped((6 * PAD, ROWS), BF16),
            shaped((4, 2 * PAD, 2 * LANES), BF16),
            shaped((4, 2 * PAD, LANES), BF16),
            shaped((LANES, 3 * LANES)),
            shaped((LANES, 3 * LANES)),
            shaped((LANES, LANES)),
        ],
        compiler_params=LIMIT,
        name="prepare_rest",
    )(
        elastic,
        interior_gradient_tables,
        jnp.transpose(surface_raise_tables, (2, 0, 1)),
        jnp.transpose(tensors, (1, 0, 2)),
        boundary_polynomials_sampled,
        quadrature_gather_weights,
        e, f, g, h, tile, side, linear, slip,
    )

    width = 2048
    block = pl.BlockSpec((64, width), lambda i: (0, i))
    depth = np.arange(64, dtype=np.float32) / 8.0
    curve = np.exp(-depth * depth)[:, None].astype(np.float32)
    new_temperature, new_pressure, top = pl.pallas_call(
        thermal_kernel,
        grid=(points // width,),
        in_specs=[
            block, block, pl.BlockSpec((1, width), lambda i: (0, i)),
            fixed((64, 1)), fixed((64, 64)), fixed((64, 64)),
        ],
        out_specs=[block, block, pl.BlockSpec((width // LANES, LANES), lambda i: (i, 0))],
        out_shape=[shaped((64, points)), shaped((64, points)), shaped((points // LANES, LANES))],
        compiler_params=LIMIT,
        name="thermal",
    )(
        thermal_field, fluid_load, earlier_sliding_speed.reshape(1, points), curve,
        sensitivity, hydraulic_diffusion_resolvent,
    )

    partial = pl.pallas_call(
        volume_kernel,
        grid=(elems // step,),
        in_specs=[column(ROWS), column(3), column(ROWS), fixed((6 * PAD, ROWS))],
        out_specs=column(ROWS),
        out_shape=shaped((ROWS, elems)),
        compiler_params=LIMIT,
        name="volume",
    )(modal_unknowns, timestep_metric_scaling, integral, mi)

    faults, partial, top = lax.optimization_barrier((rupture_side_index, partial, top))
    extent = faces_total + 3072
    payload = pl.pallas_call(
        payload_kernel,
        in_specs=whole(7, (0, 1, 2), (3, 4, 5, 6)),
        out_specs=whole(1)[0],
        out_shape=shaped((devices * 8, LANES)),
        scratch_shapes=[pltpu.VMEM((extent + 8, LANES), F32), pltpu.SemaphoreType.DMA((4,))],
        compiler_params=LIMIT,
        name="payload",
    )(faults, rupture_seat_partition, entry, face_rows, group, lower, upper)
    arrived = lax.all_to_all(payload, ("wide", "narrow"), split_axis=0, concat_axis=0, tiled=True)

    def half(first, value):
        return pl.pallas_call(
            lambda *refs: outside_kernel(first, *refs),
            in_specs=whole(8, (0,), (1, 2, 3, 4)),
            out_specs=whole(1)[0],
            out_shape=shaped((ROWS, elems)),
            scratch_shapes=[
                pltpu.VMEM((extent, LANES), F32),
                pltpu.VMEM((elems, LANES), F32),
                pltpu.SemaphoreType.DMA((4,)),
            ],
            compiler_params=LIMIT,
            name="outside" + str(first),
        )(entry, face_rows, group, lower, upper, value, open_area, wf)

    partial, payload = lax.optimization_barrier((partial, payload))
    base = half(0, partial)
    base, top = lax.optimization_barrier((base, top))
    flat = lambda x: x.reshape(points // LANES, LANES)
    imposed, rate = pl.pallas_call(
        fault_kernel,
        in_specs=whole(9),
        out_specs=whole(2),
        out_shape=[shaped((devices * 4, LANES)), shaped((points // LANES, LANES))],
        compiler_params=LIMIT,
        name="fault",
    )(
        arrived, top, flat(earlier_sliding_speed), flat(instant_sensitivity_a),
        flat(aging_memory_theta), wm, wp, vm, pair,
    )
    returned = lax.all_to_all(imposed, ("wide", "narrow"), split_axis=0, concat_axis=0, tiled=True)
    base, rate = lax.optimization_barrier((base, rate))
    base = half(2, base)

    advanced = pl.pallas_call(
        finish_kernel,
        in_specs=whole(6, (0, 1), (3,)),
        out_specs=whole(1)[0],
        out_shape=shaped((ROWS, elems)),
        scratch_shapes=[
            pltpu.VMEM((faces_total + 8, LANES), F32),
            pltpu.VMEM((ROWS, elems), F32),
            pltpu.SemaphoreType.DMA((1,)),
        ],
        compiler_params=LIMIT,
        name="finish",
    )(rupture_side_index, rupture_seat_partition, returned, base, surface_measure_quotient, ws)
    return advanced, new_temperature, new_pressure, rate.reshape(points)


def solution(mesh):
    split = P(None, ("wide", "narrow"))
    flat = P(("wide", "narrow"))
    return jax.shard_map(
        per_device,
        mesh=mesh,
        in_specs=(split,) * 3 + (P(),) * 10 + (split,) * 2 + (flat,) * 3 + (split,) * 2 + (flat,) * 2,
        out_specs=(split, split, split, flat),
        check_vma=False,
    )
```

```python
import jax
import jax.numpy as jnp
import numpy as np
from jax import lax
from jax.experimental import pallas as pl
from jax.experimental.pallas import tpu as pltpu
from jax.sharding import PartitionSpec as P

NEWTON = 4
Q, NB, NJ, NG = 9, 20, 10, 16
LANES = 128
ROWS = Q * NB
PAD = 192
HIGHEST = lax.Precision.HIGHEST
F32 = jnp.float32
BF16 = jnp.bfloat16
VMEM = pltpu.MemorySpace.VMEM
SMEM = pltpu.MemorySpace.SMEM
LIMIT = pltpu.CompilerParams(vmem_limit_bytes=56 * 1024 * 1024)


def tables():
    e = np.zeros((ROWS, Q), np.float32)
    f = np.zeros((ROWS, NB), np.float32)
    for q in range(Q):
        for b in range(NB):
            e[q * NB + b, q] = 1
            f[q * NB + b, b] = 1
    g = np.zeros((LANES, Q), np.float32)
    h = np.zeros((LANES, NJ), np.float32)
    for q in range(Q):
        for j in range(NJ):
            g[q * NJ + j, q] = 1
            h[q * NJ + j, j] = 1
    tile = np.zeros((LANES, NG), np.float32)
    for lane in range(LANES):
        tile[lane, lane % NG] = 1
    side = np.zeros((LANES, 4), np.float32)
    for q, column, low, high in ((3, 0, 0.5, 0.5), (6, 0, -0.5, 0.5), (0, 1, 0.5, 0.5), (7, 1, -0.5, 0.5)):
        side[q * NJ : (q + 1) * NJ, column] = low
        side[q * NJ : (q + 1) * NJ, 2 + column] = high
    mid = np.zeros((2, Q, Q), np.float32)
    mid[:] = 0.5 * np.eye(Q)
    mid[0, 6, 3] = -0.5
    mid[1, 6, 3] = 0.5
    linear = np.stack([g @ mid[0] @ g.T, g @ mid[1] @ g.T])
    slip = np.zeros((1, LANES), np.float32)
    slip[0, 3 * NJ : 4 * NJ] = -1.0
    slip[0, 6 * NJ : 7 * NJ] = 0.5
    pair = np.zeros((64, LANES), np.float32)
    for s in range(LANES):
        pair[s // 2, s] = 1
    return e, f, g, h, tile, side, linear, slip, pair


def dot(a, b, ca=1, cb=0, precision=HIGHEST):
    return lax.dot_general(
        a, b, (((ca,), (cb,)), ((), ())), precision=precision, preferred_element_type=F32
    )


def halves(x):
    high = x.astype(BF16)
    return high, (x - high.astype(F32)).astype(BF16)


def single(a, b, cb=0):
    return lax.dot_general(a, b, (((1,), (cb,)), ((), ())), preferred_element_type=F32)


def triple(a, b):
    ah, al = halves(a)
    bh, bl = halves(b)
    return single(ah, bh) + (single(ah, bl) + single(al, bh))


def put(out, at, value, half):
    high, low = halves(value)
    rows, lanes = value.shape
    out[at[0] + (slice(at[1], at[1] + rows), slice(at[2], at[2] + lanes))] = high
    out[at[0] + (slice(half + at[1], half + at[1] + rows), slice(at[2], at[2] + lanes))] = low


def stacked(weights, x, cb=0):
    xh, xl = halves(x)
    half = weights.shape[0] // 2
    both = single(weights, xh, cb)
    return both[0:half] + (both[half:] + single(weights[0:half], xl, cb))


def spread_rows(select, x):
    xh, xl = halves(x)
    return single(select, xh) + single(select, xl)


def grid_of(rows_of, x, lanes_of):
    return spread_rows(rows_of, dot(x, lanes_of, 1, 1))


def prepare_kernel(a, pd, rs, e, f, g, h, mp, wt):
    e_, f_, g_, h_ = e[...], f[...], g[...], h[...]
    eb, fb = e_.astype(BF16), f_.astype(BF16)
    mp[...] = jnp.zeros(mp.shape, BF16)
    for d in range(3):
        left = grid_of(eb, a[:, d, :], e_)
        put(mp, ((), d * PAD, 0), -left * grid_of(fb, pd[d], f_), 3 * PAD)
    same = single(eb, g_.astype(BF16), 1)
    for face in range(4):
        lift = spread_rows(fb, dot(rs[:, face, :], h_, 0, 1))
        high, low = halves(same * lift)
        wt[0, :, face * LANES : (face + 1) * LANES] = high
        wt[1, :, face * LANES : (face + 1) * LANES] = low


def prepare_rest_kernel(
    face, area, a, kd, sr, rt, bp, qg, e, f, g, h, tile, side, linear, slip,
    open_area, mi, wf, ws, wm, wp, vm,
):
    e_, f_, g_, h_ = e[...], f[...], g[...], h[...]
    eb, fb = e_.astype(BF16), f_.astype(BF16)
    index = face[...]
    high = lax.shift_right_arithmetic(index, 7)
    rows = lax.broadcasted_iota(jnp.int32, (64, index.shape[1]), 0)
    lanes = lax.broadcasted_iota(jnp.int32, (LANES, index.shape[1]), 0)
    upper = jnp.where(rows == high, 1.0, 0.0).astype(BF16)
    lower = jnp.where(lanes == (index & 127), 1.0, 0.0).astype(BF16)
    closed = single(upper, lower, 1)
    for r in range(64):
        at = (slice(r // 16, r // 16 + 1), slice(r % 16 * LANES, (r % 16 + 1) * LANES))
        open_area[at] = jnp.where(closed[r : r + 1] > 0.5, 0.0, area[at])
    mi[...] = jnp.zeros(mi.shape, BF16)
    wf[...] = jnp.zeros(wf.shape, BF16)
    ws[...] = jnp.zeros(ws.shape, BF16)
    for d in range(3):
        left = grid_of(eb, a[:, d, :], e_)
        put(mi, ((), d * PAD, 0), left * grid_of(fb, kd[d], f_), 3 * PAD)
    r0 = grid_of(eb, rt[:, 0, :], g_)
    r1 = grid_of(eb, rt[:, 1, :], g_)
    for n in range(4):
        lift = spread_rows(fb, dot(sr[:, n, :], h_, 0, 1))
        put(wf, ((n,), 0, 0), r0 * lift, PAD)
        put(wf, ((n,), 0, LANES), r1 * lift, PAD)
        put(ws, ((n,), 0, 0), (r0 + r1) * lift, PAD)
    hb = dot(dot(h_, bp[...], 1, 1), tile[...], 1, 1)
    hch = dot(dot(h_, dot(bp[...], qg[...], 0, 0)), h_, 1, 1)
    for out, at in ((wm, 0), (wp, 1)):
        out[:, 0:LANES] = hb * side[:, 2 * at : 2 * at + 1]
        out[:, LANES : 2 * LANES] = hb * side[:, 2 * at + 1 : 2 * at + 2]
        out[:, 2 * LANES :] = hch * linear[at]
    vm[...] = dot(dot(tile[...], qg[...]), h_, 1, 1) * slip[...]


def directional(weights, x, times):
    y = stacked(weights, x)
    return (
        y[0:ROWS] * times[0:1]
        + y[PAD : PAD + ROWS] * times[1:2]
        + y[2 * PAD : 2 * PAD + ROWS] * times[2:3]
    )


def predictor_kernel(u, t, mp, wt, integral, faces, padded):
    times = t[...]
    current = u[...]
    total = current
    factor = 1.0
    for degree in range(1, 4):
        current = directional(mp[...], current, times)
        factor = factor * (degree + 1)
        total = total + current * (1.0 / factor)
    integral[...] = total
    padded[...] = jnp.zeros(padded.shape, F32)
    padded[0:ROWS, :] = total
    xh, xl = halves(padded[...].T[:, 0:ROWS])
    rows = single(xh, wt[0]) + (single(xh, wt[1]) + single(xl, wt[0]))
    for face in range(4):
        faces[face] = rows[:, face * LANES : (face + 1) * LANES]


def volume_kernel(u, t, integral, mi, partial):
    partial[...] = u[...] + directional(mi[...], integral[...], t[...])


def take_rows(index, row, source, target, base):
    def body(i, carry):
        first = pl.multiple_of(i * LANES, LANES)
        listed = index.at[row, pl.ds(first, LANES)]
        place = target.at[pl.ds(base + first, LANES)]
        for at in range(0, LANES, 16):
            rows = [source[pl.ds(listed[at + k], 1), :] for k in range(16)]
            for k in range(16):
                place[at + k : at + k + 1, :] = rows[k]
        return carry

    lax.fori_loop(0, index.shape[1] // LANES, body, 0)


def send_kernel(index, faces, group, lower, upper):
    for peer in range(4):
        take_rows(index, peer, faces, group, peer * index.shape[1])
    take_rows(index, 4, faces, lower, 0)
    take_rows(index, 5, faces, upper, 0)


def thermal_kernel(th, fl, speed, shape, tr, hr, new_th, new_fl, top):
    v = speed[...]
    old = th[...]
    warmed = old + shape[...] * (0.5 * v * v)
    fresh = stacked(jnp.concatenate(halves(tr[...]), axis=0), warmed)
    new_th[...] = fresh
    pressure = stacked(jnp.concatenate(halves(hr[...]), axis=0), fl[...] + 0.5 * (fresh - old))
    new_fl[...] = pressure
    for r in range(top.shape[0]):
        top[r : r + 1, :] = pressure[0:1, r * LANES : (r + 1) * LANES]


def fill(table, parts, sems):
    at = 0
    copies = []
    for i, part in enumerate(parts):
        rows = part.shape[0]
        copies.append(pltpu.make_async_copy(part, table.at[pl.ds(at, rows)], sems.at[i]))
        at += rows
    for copy in copies:
        copy.start()
    for copy in copies:
        copy.wait()


def live_blocks(seat):
    return lax.fori_loop(
        0, seat.shape[0] // 4, lambda i, c: c + (seat[i * 4] >= 0).astype(jnp.int32), 0
    )


def payload_kernel(face, seat, entry, faces, group, lower, upper, payload, table, sems):
    extent = table.shape[0] - 8
    payload[...] = jnp.zeros(payload.shape, F32)
    table[extent : extent + 8, :] = jnp.zeros((8, LANES), F32)
    blocks = live_blocks(seat)
    fill(table, (faces, group, lower, upper), sems)

    def body(i, carry):
        owner = seat[i * 4]
        rows = []
        for k in range(4):
            column = face[i * 4 + k]
            live = column >= 0
            rows.append(table[pl.ds(jnp.where(live, column, extent), 1), :])
            safe = jnp.maximum(column, 0)
            outer = entry[lax.shift_right_logical(safe, 11), safe & 2047]
            outer = jnp.where(live, outer, extent)
            rows.append(table[pl.ds(outer, 1), :])
        for k in range(4):
            payload[pl.ds(owner * 8 + k, 1), :] = rows[2 * k]
            payload[pl.ds(owner * 8 + 4 + k, 1), :] = rows[2 * k + 1]
        return carry

    lax.fori_loop(0, blocks, body, 0)


def outside_kernel(first, entry, faces, group, lower, upper, partial, area, wf, base, table, outside, sems):
    fill(table, (faces, group, lower, upper), sems)
    elems = faces.shape[0] // 4
    result = partial[...]
    for face in (first, first + 1):
        take_rows(entry, face, table, outside, 0)
        rows = jnp.concatenate([table[face * elems : (face + 1) * elems, :], outside[...]], axis=1)
        flux = stacked(wf[face], rows, 1)
        result = result - flux[0:ROWS] * area[face : face + 1, :]
    base[...] = result


def fault_kernel(arrived, top, speed, sense, memory, wm, wp, vm, pair, imposed, rate):
    lanes = lax.shift_right_logical(lax.broadcasted_iota(jnp.int32, (LANES, LANES), 1), 4)
    half = (lax.broadcasted_iota(jnp.int32, (LANES, LANES), 0) & 1) * 4
    pick = lambda at: jnp.concatenate(
        [arrived[pl.ds(at + k, LANES, stride=8), :] for k in range(4)], axis=0
    )
    linear = triple(pick(0), wm[...]) + triple(pick(4), wp[...])
    locked = jnp.zeros((LANES, LANES), F32)
    normal = jnp.zeros((LANES, LANES), F32)
    for k in range(4):
        mine = lanes == half + k
        part = linear[k * LANES : (k + 1) * LANES]
        locked = locked + jnp.where(mine, part[:, 0:LANES], 0.0)
        normal = normal + jnp.where(mine, part[:, LANES : 2 * LANES], 0.0)
    locked = dot(pair[...], locked)
    normal = dot(pair[...], normal)
    excess = 2.0 + normal - top[...]
    effective = jnp.maximum(excess, 0.0) + jnp.log1p(jnp.exp(-jnp.abs(excess)))
    strength = effective * sense[...]
    weight = 0.5 * jnp.exp(memory[...] / sense[...])
    v = speed[...]
    for _ in range(NEWTON):
        scaled = weight * v
        root = jnp.sqrt(1.0 + scaled * scaled)
        size = jnp.log(jnp.abs(scaled) + root)
        mismatch = locked - v - strength * jnp.where(scaled < 0.0, -size, size)
        slope = -1.0 - strength * weight / root
        v = v - mismatch / slope
    rate[...] = v
    spread = dot(pair[...], v, 0, 0)
    mine = jnp.concatenate(
        [jnp.where(lanes == half + k, spread, 0.0) for k in range(4)], axis=0
    )
    result = linear[:, 2 * LANES :] + triple(mine, vm[...])
    for k in range(4):
        imposed[pl.ds(k, LANES, stride=4), :] = result[k * LANES : (k + 1) * LANES]


def finish_kernel(face, seat, returned, base, area, ws, out, spread, held, sems):
    copy = pltpu.make_async_copy(base, held, sems.at[0])
    copy.start()
    count = spread.shape[0] - 8
    elems = count // 4
    spread[...] = jnp.zeros(spread.shape, F32)

    def body(i, carry):
        owner = seat[i * 4]
        rows = [returned[pl.ds(owner * 4 + k, 1), :] for k in range(4)]
        for k in range(4):
            column = face[i * 4 + k]
            spread[pl.ds(jnp.where(column >= 0, column, count), 1), :] = rows[k]
        return carry

    lax.fori_loop(0, live_blocks(seat), body, 0)
    copy.wait()
    result = held[...]
    for at in range(4):
        flux = stacked(ws[at], spread[at * elems : (at + 1) * elems, :], 1)
        result = result - flux[0:ROWS] * area[at : at + 1, :]
    out[...] = result


def shaped(shape, dtype=F32):
    return jax.ShapeDtypeStruct(shape, dtype)


def whole(count, smem=(), left=()):
    space = lambda i: SMEM if i in smem else pl.ANY if i in left else VMEM
    return [pl.BlockSpec(memory_space=space(i)) for i in range(count)]


def shift(array, axis, by):
    peers = lax.axis_size(axis)
    pairs = [(i, i + by) for i in range(peers) if 0 <= i + by < peers]
    return lax.ppermute(array, axis, pairs)


def per_device(
    modal_unknowns,
    timestep_metric_scaling,
    surface_measure_quotient,
    elastic_directional_derivs,
    predictor_derivatives,
    interior_gradient_tables,
    interior_restriction,
    surface_raise_tables,
    riemann_numerical_tables,
    boundary_polynomials_sampled,
    quadrature_gather_weights,
    thermal_diffusion_resolvent,
    hydraulic_diffusion_resolvent,
    thermal_field,
    fluid_load,
    earlier_sliding_speed,
    instant_sensitivity_a,
    aging_memory_theta,
    outbound_ghost_indices,
    boundary_entry_index,
    rupture_side_index,
    rupture_seat_partition,
):
    elems = modal_unknowns.shape[1]
    faces_total = 4 * elems
    devices = lax.axis_size(("wide", "narrow"))
    points = thermal_field.shape[1]
    e, f, g, h, tile, side, linear, slip, pair = tables()
    entry = boundary_entry_index
    elastic = jnp.transpose(elastic_directional_derivs, (1, 0, 2))

    mp, wt = pl.pallas_call(
        prepare_kernel,
        in_specs=whole(7),
        out_specs=whole(2),
        out_shape=[shaped((6 * PAD, ROWS), BF16), shaped((2, ROWS, 4 * LANES), BF16)],
        compiler_params=LIMIT,
        name="prepare",
    )(
        elastic, predictor_derivatives, jnp.transpose(interior_restriction, (1, 0, 2)), e, f, g, h
    )

    step = 512
    column = lambda rows: pl.BlockSpec((rows, step), lambda i: (0, i))
    fixed = lambda shape: pl.BlockSpec(shape, lambda i: (0,) * len(shape))
    integral, face_rows = pl.pallas_call(
        predictor_kernel,
        grid=(elems // step,),
        in_specs=[column(ROWS), column(3), fixed((6 * PAD, ROWS)), fixed((2, ROWS, 4 * LANES))],
        out_specs=[column(ROWS), pl.BlockSpec((4, step, LANES), lambda i: (0, i, 0))],
        out_shape=[shaped((ROWS, elems)), shaped((4, elems, LANES))],
        scratch_shapes=[pltpu.VMEM((256, step), F32)],
        compiler_params=LIMIT,
        name="predictor",
    )(modal_unknowns, timestep_metric_scaling, mp, wt)
    face_rows = face_rows.reshape(faces_total, LANES)

    group_out, lower_out, upper_out = pl.pallas_call(
        send_kernel,
        in_specs=whole(2, (0,)),
        out_specs=whole(3),
        out_shape=[shaped((2048, LANES)), shaped((512, LANES)), shaped((512, LANES))],
        compiler_params=LIMIT,
        name="halo_rows",
    )(outbound_ghost_indices, face_rows)
    group = lax.all_to_all(group_out, "narrow", split_axis=0, concat_axis=0, tiled=True)
    lower = shift(lower_out, "wide", 1)
    upper = shift(upper_out, "wide", -1)

    tensors, sensitivity, _ = lax.optimization_barrier(
        (riemann_numerical_tables, thermal_diffusion_resolvent, lower_out)
    )
    open_area, mi, wf, ws, wm, wp, vm = pl.pallas_call(
        prepare_rest_kernel,
        in_specs=whole(16),
        out_specs=whole(7),
        out_shape=[
            shaped((4, elems)),
            shaped((6 * PAD, ROWS), BF16),
            shaped((4, 2 * PAD, 2 * LANES), BF16),
            shaped((4, 2 * PAD, LANES), BF16),
            shaped((LANES, 3 * LANES)),
            shaped((LANES, 3 * LANES)),
            shaped((LANES, LANES)),
        ],
        compiler_params=LIMIT,
        name="prepare_rest",
    )(
        rupture_side_index.reshape(1, -1),
        surface_measure_quotient,
        elastic,
        interior_gradient_tables,
        jnp.transpose(surface_raise_tables, (2, 0, 1)),
        jnp.transpose(tensors, (1, 0, 2)),
        boundary_polynomials_sampled,
        quadrature_gather_weights,
        e, f, g, h, tile, side, linear, slip,
    )

    width = 2048
    block = pl.BlockSpec((64, width), lambda i: (0, i))
    depth = np.arange(64, dtype=np.float32) / 8.0
    curve = np.exp(-depth * depth)[:, None].astype(np.float32)
    new_temperature, new_pressure, top = pl.pallas_call(
        thermal_kernel,
        grid=(points // width,),
        in_specs=[
            block, block, pl.BlockSpec((1, width), lambda i: (0, i)),
            fixed((64, 1)), fixed((64, 64)), fixed((64, 64)),
        ],
        out_specs=[block, block, pl.BlockSpec((width // LANES, LANES), lambda i: (i, 0))],
        out_shape=[shaped((64, points)), shaped((64, points)), shaped((points // LANES, LANES))],
        compiler_params=LIMIT,
        name="thermal",
    )(
        thermal_field, fluid_load, earlier_sliding_speed.reshape(1, points), curve,
        sensitivity, hydraulic_diffusion_resolvent,
    )

    partial = pl.pallas_call(
        volume_kernel,
        grid=(elems // step,),
        in_specs=[column(ROWS), column(3), column(ROWS), fixed((6 * PAD, ROWS))],
        out_specs=column(ROWS),
        out_shape=shaped((ROWS, elems)),
        compiler_params=LIMIT,
        name="volume",
    )(modal_unknowns, timestep_metric_scaling, integral, mi)

    faults, partial, top = lax.optimization_barrier((rupture_side_index, partial, top))
    extent = faces_total + 3072
    payload = pl.pallas_call(
        payload_kernel,
        in_specs=whole(7, (0, 1, 2), (3, 4, 5, 6)),
        out_specs=whole(1)[0],
        out_shape=shaped((devices * 8, LANES)),
        scratch_shapes=[pltpu.VMEM((extent + 8, LANES), F32), pltpu.SemaphoreType.DMA((4,))],
        compiler_params=LIMIT,
        name="payload",
    )(faults, rupture_seat_partition, entry, face_rows, group, lower, upper)
    arrived = lax.all_to_all(payload, ("wide", "narrow"), split_axis=0, concat_axis=0, tiled=True)

    def half(first, value):
        return pl.pallas_call(
            lambda *refs: outside_kernel(first, *refs),
            in_specs=whole(8, (0,), (1, 2, 3, 4)),
            out_specs=whole(1)[0],
            out_shape=shaped((ROWS, elems)),
            scratch_shapes=[
                pltpu.VMEM((extent, LANES), F32),
                pltpu.VMEM((elems, LANES), F32),
                pltpu.SemaphoreType.DMA((4,)),
            ],
            compiler_params=LIMIT,
            name="outside" + str(first),
        )(entry, face_rows, group, lower, upper, value, open_area, wf)

    partial, payload = lax.optimization_barrier((partial, payload))
    base = half(0, partial)
    base, top = lax.optimization_barrier((base, top))
    flat = lambda x: x.reshape(points // LANES, LANES)
    imposed, rate = pl.pallas_call(
        fault_kernel,
        in_specs=whole(9),
        out_specs=whole(2),
        out_shape=[shaped((devices * 4, LANES)), shaped((points // LANES, LANES))],
        compiler_params=LIMIT,
        name="fault",
    )(
        arrived, top, flat(earlier_sliding_speed), flat(instant_sensitivity_a),
        flat(aging_memory_theta), wm, wp, vm, pair,
    )
    returned = lax.all_to_all(imposed, ("wide", "narrow"), split_axis=0, concat_axis=0, tiled=True)
    base, rate = lax.optimization_barrier((base, rate))
    base = half(2, base)

    advanced = pl.pallas_call(
        finish_kernel,
        in_specs=whole(6, (0, 1), (3,)),
        out_specs=whole(1)[0],
        out_shape=shaped((ROWS, elems)),
        scratch_shapes=[
            pltpu.VMEM((faces_total + 8, LANES), F32),
            pltpu.VMEM((ROWS, elems), F32),
            pltpu.SemaphoreType.DMA((1,)),
        ],
        compiler_params=LIMIT,
        name="finish",
    )(rupture_side_index, rupture_seat_partition, returned, base, surface_measure_quotient, ws)
    return advanced, new_temperature, new_pressure, rate.reshape(points)


def solution(mesh):
    split = P(None, ("wide", "narrow"))
    flat = P(("wide", "narrow"))
    return jax.shard_map(
        per_device,
        mesh=mesh,
        in_specs=(split,) * 3 + (P(),) * 10 + (split,) * 2 + (flat,) * 3 + (split,) * 2 + (flat,) * 2,
        out_specs=(split, split, split, flat),
        check_vma=False,
    )
```

```python
import jax
import jax.numpy as jnp
import numpy as np
from jax import lax
from jax.experimental import pallas as pl
from jax.experimental.pallas import tpu as pltpu
from jax.sharding import PartitionSpec as P

NEWTON = 4
Q, NB, NJ, NG = 9, 20, 10, 16
LANES = 128
ROWS = Q * NB
PAD = 192
HIGHEST = lax.Precision.HIGHEST
F32 = jnp.float32
BF16 = jnp.bfloat16
VMEM = pltpu.MemorySpace.VMEM
SMEM = pltpu.MemorySpace.SMEM
LIMIT = pltpu.CompilerParams(vmem_limit_bytes=24 * 1024 * 1024)


def tables():
    e = np.zeros((ROWS, Q), np.float32)
    f = np.zeros((ROWS, NB), np.float32)
    for q in range(Q):
        for b in range(NB):
            e[q * NB + b, q] = 1
            f[q * NB + b, b] = 1
    g = np.zeros((LANES, Q), np.float32)
    h = np.zeros((LANES, NJ), np.float32)
    for q in range(Q):
        for j in range(NJ):
            g[q * NJ + j, q] = 1
            h[q * NJ + j, j] = 1
    tile = np.zeros((LANES, NG), np.float32)
    for lane in range(LANES):
        tile[lane, lane % NG] = 1
    side = np.zeros((LANES, 4), np.float32)
    for q, column, low, high in ((3, 0, 0.5, 0.5), (6, 0, -0.5, 0.5), (0, 1, 0.5, 0.5), (7, 1, -0.5, 0.5)):
        side[q * NJ : (q + 1) * NJ, column] = low
        side[q * NJ : (q + 1) * NJ, 2 + column] = high
    mid = np.zeros((2, Q, Q), np.float32)
    mid[:] = 0.5 * np.eye(Q)
    mid[0, 6, 3] = -0.5
    mid[1, 6, 3] = 0.5
    linear = np.stack([g @ mid[0] @ g.T, g @ mid[1] @ g.T])
    slip = np.zeros((1, LANES), np.float32)
    slip[0, 3 * NJ : 4 * NJ] = -1.0
    slip[0, 6 * NJ : 7 * NJ] = 0.5
    pair = np.zeros((64, LANES), np.float32)
    for s in range(LANES):
        pair[s // 2, s] = 1
    return e, f, g, h, tile, side, linear, slip, pair


def dot(a, b, ca=1, cb=0, precision=HIGHEST):
    return lax.dot_general(
        a, b, (((ca,), (cb,)), ((), ())), precision=precision, preferred_element_type=F32
    )


def halves(x):
    high = x.astype(BF16)
    return high, (x - high.astype(F32)).astype(BF16)


def single(a, b, cb=0):
    return lax.dot_general(a, b, (((1,), (cb,)), ((), ())), preferred_element_type=F32)


def triple(a, b):
    ah, al = halves(a)
    bh, bl = halves(b)
    return single(ah, bh) + (single(ah, bl) + single(al, bh))


def put(out, at, value, half):
    high, low = halves(value)
    rows, lanes = value.shape
    out[at[0] + (slice(at[1], at[1] + rows), slice(at[2], at[2] + lanes))] = high
    out[at[0] + (slice(half + at[1], half + at[1] + rows), slice(at[2], at[2] + lanes))] = low


def stacked(weights, x, cb=0):
    xh, xl = halves(x)
    half = weights.shape[0] // 2
    both = single(weights, xh, cb)
    return both[0:half] + (both[half:] + single(weights[0:half], xl, cb))


def spread_rows(select, x):
    xh, xl = halves(x)
    return single(select, xh) + single(select, xl)


def grid_of(rows_of, x, lanes_of):
    return spread_rows(rows_of, dot(x, lanes_of, 1, 1))


def prepare_kernel(a, pd, rs, e, f, g, h, mp, wt):
    e_, f_, g_, h_ = e[...], f[...], g[...], h[...]
    eb, fb = e_.astype(BF16), f_.astype(BF16)
    mp[...] = jnp.zeros(mp.shape, BF16)
    for d in range(3):
        left = grid_of(eb, a[:, d, :], e_)
        put(mp, ((), d * PAD, 0), -left * grid_of(fb, pd[d], f_), 3 * PAD)
    same = single(eb, g_.astype(BF16), 1)
    for face in range(4):
        lift = spread_rows(fb, dot(rs[:, face, :], h_, 0, 1))
        high, low = halves(same * lift)
        wt[0, :, face * LANES : (face + 1) * LANES] = high
        wt[1, :, face * LANES : (face + 1) * LANES] = low


def prepare_rest_kernel(
    face, area, a, kd, sr, rt, bp, qg, e, f, g, h, tile, side, linear, slip,
    open_area, mi, wf, ws, wm, wp, vm,
):
    e_, f_, g_, h_ = e[...], f[...], g[...], h[...]
    eb, fb = e_.astype(BF16), f_.astype(BF16)
    index = face[...]
    high = lax.shift_right_arithmetic(index, 7)
    rows = lax.broadcasted_iota(jnp.int32, (64, index.shape[1]), 0)
    lanes = lax.broadcasted_iota(jnp.int32, (LANES, index.shape[1]), 0)
    upper = jnp.where(rows == high, 1.0, 0.0).astype(BF16)
    lower = jnp.where(lanes == (index & 127), 1.0, 0.0).astype(BF16)
    closed = single(upper, lower, 1)
    for r in range(64):
        at = (slice(r // 16, r // 16 + 1), slice(r % 16 * LANES, (r % 16 + 1) * LANES))
        open_area[at] = jnp.where(closed[r : r + 1] > 0.5, 0.0, area[at])
    mi[...] = jnp.zeros(mi.shape, BF16)
    wf[...] = jnp.zeros(wf.shape, BF16)
    ws[...] = jnp.zeros(ws.shape, BF16)
    for d in range(3):
        left = grid_of(eb, a[:, d, :], e_)
        put(mi, ((), d * PAD, 0), left * grid_of(fb, kd[d], f_), 3 * PAD)
    r0 = grid_of(eb, rt[:, 0, :], g_)
    r1 = grid_of(eb, rt[:, 1, :], g_)
    for n in range(4):
        lift = spread_rows(fb, dot(sr[:, n, :], h_, 0, 1))
        put(wf, ((n,), 0, 0), r0 * lift, PAD)
        put(wf, ((n,), 0, LANES), r1 * lift, PAD)
        put(ws, ((n,), 0, 0), (r0 + r1) * lift, PAD)
    hb = dot(dot(h_, bp[...], 1, 1), tile[...], 1, 1)
    hch = dot(dot(h_, dot(bp[...], qg[...], 0, 0)), h_, 1, 1)
    for out, at in ((wm, 0), (wp, 1)):
        out[:, 0:LANES] = hb * side[:, 2 * at : 2 * at + 1]
        out[:, LANES : 2 * LANES] = hb * side[:, 2 * at + 1 : 2 * at + 2]
        out[:, 2 * LANES :] = hch * linear[at]
    vm[...] = dot(dot(tile[...], qg[...]), h_, 1, 1) * slip[...]


def directional(weights, x, times):
    y = stacked(weights, x)
    return (
        y[0:ROWS] * times[0:1]
        + y[PAD : PAD + ROWS] * times[1:2]
        + y[2 * PAD : 2 * PAD + ROWS] * times[2:3]
    )


def predictor_kernel(u, t, mp, wt, integral, faces, padded):
    times = t[...]
    current = u[...]
    total = current
    factor = 1.0
    for degree in range(1, 4):
        current = directional(mp[...], current, times)
        factor = factor * (degree + 1)
        total = total + current * (1.0 / factor)
    integral[...] = total
    padded[...] = jnp.zeros(padded.shape, F32)
    padded[0:ROWS, :] = total
    xh, xl = halves(padded[...].T[:, 0:ROWS])
    rows = single(xh, wt[0]) + (single(xh, wt[1]) + single(xl, wt[0]))
    for face in range(4):
        faces[face] = rows[:, face * LANES : (face + 1) * LANES]


def volume_kernel(u, t, integral, mi, partial):
    partial[...] = u[...] + directional(mi[...], integral[...], t[...])


def take_rows(index, row, source, target, base):
    def body(i, carry):
        first = pl.multiple_of(i * LANES, LANES)
        listed = index.at[row, pl.ds(first, LANES)]
        place = target.at[pl.ds(base + first, LANES)]
        for at in range(0, LANES, 16):
            rows = [source[pl.ds(listed[at + k], 1), :] for k in range(16)]
            for k in range(16):
                place[at + k : at + k + 1, :] = rows[k]
        return carry

    lax.fori_loop(0, index.shape[1] // LANES, body, 0)


def send_kernel(index, faces, group, lower, upper):
    for peer in range(4):
        take_rows(index, peer, faces, group, peer * index.shape[1])
    take_rows(index, 4, faces, lower, 0)
    take_rows(index, 5, faces, upper, 0)


def thermal_kernel(th, fl, speed, shape, tr, hr, new_th, new_fl, top):
    v = speed[...]
    old = th[...]
    warmed = old + shape[...] * (0.5 * v * v)
    fresh = stacked(jnp.concatenate(halves(tr[...]), axis=0), warmed)
    new_th[...] = fresh
    pressure = stacked(jnp.concatenate(halves(hr[...]), axis=0), fl[...] + 0.5 * (fresh - old))
    new_fl[...] = pressure
    for r in range(top.shape[0]):
        top[r : r + 1, :] = pressure[0:1, r * LANES : (r + 1) * LANES]


def fill(table, parts, sems):
    at = 0
    copies = []
    for i, part in enumerate(parts):
        rows = part.shape[0]
        copies.append(pltpu.make_async_copy(part, table.at[pl.ds(at, rows)], sems.at[i]))
        at += rows
    for copy in copies:
        copy.start()
    for copy in copies:
        copy.wait()


def live_blocks(seat):
    return lax.fori_loop(
        0, seat.shape[0] // 4, lambda i, c: c + (seat[i * 4] >= 0).astype(jnp.int32), 0
    )


def payload_kernel(face, seat, entry, faces, group, lower, upper, payload, table, buffer, sems):
    extent = table.shape[0] - 8
    buffer[...] = jnp.zeros(buffer.shape, F32)
    table[extent : extent + 8, :] = jnp.zeros((8, LANES), F32)
    blocks = live_blocks(seat)
    fill(table, (faces, group, lower, upper), sems)
    spare = buffer.shape[0] - 8

    def body(i, carry):
        rows = []
        for k in range(16):
            column = face[i * 16 + k]
            live = column >= 0
            safe = jnp.maximum(column, 0)
            outer = entry[lax.shift_right_logical(safe, 11), safe & 2047]
            rows.append(table[pl.ds(jnp.where(live, column, extent), 1), :])
            rows.append(table[pl.ds(jnp.where(live, outer, extent), 1), :])
        for n in range(4):
            owner = seat[i * 16 + n * 4]
            first = jnp.where(owner >= 0, owner * 8, spare)
            for k in range(4):
                buffer[pl.ds(first + k, 1), :] = rows[8 * n + 2 * k]
                buffer[pl.ds(first + 4 + k, 1), :] = rows[8 * n + 2 * k + 1]
        return carry

    lax.fori_loop(0, lax.shift_right_logical(blocks + 3, 2), body, 0)
    copy = pltpu.make_async_copy(buffer.at[pl.ds(0, spare)], payload, sems.at[0])
    copy.start()
    copy.wait()


def outside_kernel(first, entry, table, partial, area, wf, base, outside, held, weights, sems):
    copies = (
        pltpu.make_async_copy(wf.at[pl.ds(first, 2)], weights, sems.at[0]),
        pltpu.make_async_copy(partial, held, sems.at[1]),
    )
    for copy in copies:
        copy.start()
    elems = outside.shape[0]
    result = None
    for n in range(2):
        face = first + n
        take_rows(entry, face, table, outside, 0)
        rows = jnp.concatenate([table[face * elems : (face + 1) * elems, :], outside[...]], axis=1)
        if n == 0:
            for copy in copies:
                copy.wait()
            result = held[...]
        flux = stacked(weights[n], rows, 1)
        result = result - flux[0:ROWS] * area[face : face + 1, :]
    base[...] = result


def fault_kernel(arrived, top, speed, sense, memory, wm, wp, vm, pair, imposed, rate):
    lanes = lax.shift_right_logical(lax.broadcasted_iota(jnp.int32, (LANES, LANES), 1), 4)
    half = (lax.broadcasted_iota(jnp.int32, (LANES, LANES), 0) & 1) * 4
    pick = lambda at: jnp.concatenate(
        [arrived[pl.ds(at + k, LANES, stride=8), :] for k in range(4)], axis=0
    )
    linear = triple(pick(0), wm[...]) + triple(pick(4), wp[...])
    locked = jnp.zeros((LANES, LANES), F32)
    normal = jnp.zeros((LANES, LANES), F32)
    for k in range(4):
        mine = lanes == half + k
        part = linear[k * LANES : (k + 1) * LANES]
        locked = locked + jnp.where(mine, part[:, 0:LANES], 0.0)
        normal = normal + jnp.where(mine, part[:, LANES : 2 * LANES], 0.0)
    locked = dot(pair[...], locked)
    normal = dot(pair[...], normal)
    excess = 2.0 + normal - top[...]
    effective = jnp.maximum(excess, 0.0) + jnp.log1p(jnp.exp(-jnp.abs(excess)))
    strength = effective * sense[...]
    weight = 0.5 * jnp.exp(memory[...] / sense[...])
    v = speed[...]
    for _ in range(NEWTON):
        scaled = weight * v
        root = jnp.sqrt(1.0 + scaled * scaled)
        size = jnp.log(jnp.abs(scaled) + root)
        mismatch = locked - v - strength * jnp.where(scaled < 0.0, -size, size)
        slope = -1.0 - strength * weight / root
        v = v - mismatch / slope
    rate[...] = v
    spread = dot(pair[...], v, 0, 0)
    mine = jnp.concatenate(
        [jnp.where(lanes == half + k, spread, 0.0) for k in range(4)], axis=0
    )
    result = linear[:, 2 * LANES :] + triple(mine, vm[...])
    for k in range(4):
        imposed[pl.ds(k, LANES, stride=4), :] = result[k * LANES : (k + 1) * LANES]


def finish_kernel(face, seat, returned, base, area, ws, out, spread, held, sems):
    copy = pltpu.make_async_copy(base, held, sems.at[0])
    copy.start()
    count = spread.shape[0] - 8
    elems = count // 4
    spread[...] = jnp.zeros(spread.shape, F32)

    def body(i, carry):
        rows = []
        for n in range(4):
            owner = jnp.maximum(seat[i * 16 + n * 4], 0)
            rows += [returned[pl.ds(owner * 4 + k, 1), :] for k in range(4)]
        for k in range(16):
            column = face[i * 16 + k]
            spread[pl.ds(jnp.where(column >= 0, column, count), 1), :] = rows[k]
        return carry

    lax.fori_loop(0, lax.shift_right_logical(live_blocks(seat) + 3, 2), body, 0)
    copy.wait()
    result = held[...]
    for at in range(4):
        flux = stacked(ws[at], spread[at * elems : (at + 1) * elems, :], 1)
        result = result - flux[0:ROWS] * area[at : at + 1, :]
    out[...] = result


def shaped(shape, dtype=F32):
    return jax.ShapeDtypeStruct(shape, dtype)


def whole(count, smem=(), left=()):
    space = lambda i: SMEM if i in smem else pl.ANY if i in left else VMEM
    return [pl.BlockSpec(memory_space=space(i)) for i in range(count)]


def local(array):
    return pltpu.with_memory_space_constraint(array, VMEM)


def shift(array, axis, by):
    peers = lax.axis_size(axis)
    pairs = [(i, i + by) for i in range(peers) if 0 <= i + by < peers]
    return lax.ppermute(array, axis, pairs)


def per_device(
    modal_unknowns,
    timestep_metric_scaling,
    surface_measure_quotient,
    elastic_directional_derivs,
    predictor_derivatives,
    interior_gradient_tables,
    interior_restriction,
    surface_raise_tables,
    riemann_numerical_tables,
    boundary_polynomials_sampled,
    quadrature_gather_weights,
    thermal_diffusion_resolvent,
    hydraulic_diffusion_resolvent,
    thermal_field,
    fluid_load,
    earlier_sliding_speed,
    instant_sensitivity_a,
    aging_memory_theta,
    outbound_ghost_indices,
    boundary_entry_index,
    rupture_side_index,
    rupture_seat_partition,
):
    elems = modal_unknowns.shape[1]
    faces_total = 4 * elems
    devices = lax.axis_size(("wide", "narrow"))
    points = thermal_field.shape[1]
    e, f, g, h, tile, side, linear, slip, pair = tables()
    entry = boundary_entry_index
    elastic = jnp.transpose(elastic_directional_derivs, (1, 0, 2))

    mp, wt = pl.pallas_call(
        prepare_kernel,
        in_specs=whole(7),
        out_specs=whole(2),
        out_shape=[shaped((6 * PAD, ROWS), BF16), shaped((2, ROWS, 4 * LANES), BF16)],
        compiler_params=LIMIT,
        name="prepare",
    )(
        elastic, predictor_derivatives, jnp.transpose(interior_restriction, (1, 0, 2)), e, f, g, h
    )

    step = 512
    column = lambda rows: pl.BlockSpec((rows, step), lambda i: (0, i))
    fixed = lambda shape: pl.BlockSpec(shape, lambda i: (0,) * len(shape))
    integral, face_rows = pl.pallas_call(
        predictor_kernel,
        grid=(elems // step,),
        in_specs=[column(ROWS), column(3), fixed((6 * PAD, ROWS)), fixed((2, ROWS, 4 * LANES))],
        out_specs=[column(ROWS), pl.BlockSpec((4, step, LANES), lambda i: (0, i, 0))],
        out_shape=[shaped((ROWS, elems)), shaped((4, elems, LANES))],
        scratch_shapes=[pltpu.VMEM((256, step), F32)],
        compiler_params=LIMIT,
        name="predictor",
    )(modal_unknowns, timestep_metric_scaling, mp, wt)
    face_rows = face_rows.reshape(faces_total, LANES)

    group_out, lower_out, upper_out = pl.pallas_call(
        send_kernel,
        in_specs=whole(2, (0,)),
        out_specs=whole(3),
        out_shape=[shaped((2048, LANES)), shaped((512, LANES)), shaped((512, LANES))],
        compiler_params=LIMIT,
        name="halo_rows",
    )(outbound_ghost_indices, face_rows)
    group = lax.all_to_all(group_out, "narrow", split_axis=0, concat_axis=0, tiled=True)
    lower = shift(lower_out, "wide", 1)
    upper = shift(upper_out, "wide", -1)

    tensors, sensitivity, _ = lax.optimization_barrier(
        (riemann_numerical_tables, thermal_diffusion_resolvent, lower_out)
    )
    open_area, mi, wf, ws, wm, wp, vm = pl.pallas_call(
        prepare_rest_kernel,
        in_specs=whole(16),
        out_specs=whole(7),
        out_shape=[
            shaped((4, elems)),
            shaped((6 * PAD, ROWS), BF16),
            shaped((4, 2 * PAD, 2 * LANES), BF16),
            shaped((4, 2 * PAD, LANES), BF16),
            shaped((LANES, 3 * LANES)),
            shaped((LANES, 3 * LANES)),
            shaped((LANES, LANES)),
        ],
        compiler_params=LIMIT,
        name="prepare_rest",
    )(
        rupture_side_index.reshape(1, -1),
        surface_measure_quotient,
        elastic,
        interior_gradient_tables,
        jnp.transpose(surface_raise_tables, (2, 0, 1)),
        jnp.transpose(tensors, (1, 0, 2)),
        boundary_polynomials_sampled,
        quadrature_gather_weights,
        e, f, g, h, tile, side, linear, slip,
    )

    width = 2048
    block = pl.BlockSpec((64, width), lambda i: (0, i))
    depth = np.arange(64, dtype=np.float32) / 8.0
    curve = np.exp(-depth * depth)[:, None].astype(np.float32)
    new_temperature, new_pressure, top = pl.pallas_call(
        thermal_kernel,
        grid=(points // width,),
        in_specs=[
            block, block, pl.BlockSpec((1, width), lambda i: (0, i)),
            fixed((64, 1)), fixed((64, 64)), fixed((64, 64)),
        ],
        out_specs=[block, block, pl.BlockSpec((width // LANES, LANES), lambda i: (i, 0))],
        out_shape=[shaped((64, points)), shaped((64, points)), shaped((points // LANES, LANES))],
        compiler_params=LIMIT,
        name="thermal",
    )(
        thermal_field, fluid_load, earlier_sliding_speed.reshape(1, points), curve,
        sensitivity, hydraulic_diffusion_resolvent,
    )

    partial = pl.pallas_call(
        volume_kernel,
        grid=(elems // step,),
        in_specs=[column(ROWS), column(3), column(ROWS), fixed((6 * PAD, ROWS))],
        out_specs=column(ROWS),
        out_shape=shaped((ROWS, elems)),
        compiler_params=LIMIT,
        name="volume",
    )(modal_unknowns, timestep_metric_scaling, integral, mi)

    faults, partial, top = lax.optimization_barrier((rupture_side_index, partial, top))
    extent = faces_total + 3072
    payload, table = pl.pallas_call(
        payload_kernel,
        in_specs=whole(7, (0, 1, 2), (3, 4, 5, 6)),
        out_specs=whole(2, (), (0,)),
        out_shape=[shaped((devices * 8, LANES)), pltpu.VMEM((extent + 8, LANES), F32)],
        scratch_shapes=[pltpu.VMEM((devices * 8 + 8, LANES), F32), pltpu.SemaphoreType.DMA((4,))],
        compiler_params=LIMIT,
        name="payload",
    )(faults, rupture_seat_partition, entry, face_rows, local(group), local(lower), local(upper))
    arrived = lax.all_to_all(payload, ("wide", "narrow"), split_axis=0, concat_axis=0, tiled=True)

    entry = boundary_entry_index

    def half(first, value):
        return pl.pallas_call(
            lambda *refs: outside_kernel(first, *refs),
            in_specs=whole(5, (0,), (2, 4)),
            out_specs=whole(1)[0],
            out_shape=shaped((ROWS, elems)),
            scratch_shapes=[
                pltpu.VMEM((elems, LANES), F32),
                pltpu.VMEM((ROWS, elems), F32),
                pltpu.VMEM((2, 2 * PAD, 2 * LANES), BF16),
                pltpu.SemaphoreType.DMA((2,)),
            ],
            compiler_params=LIMIT,
            name="outside" + str(first),
        )(entry, local(table), value, open_area, wf)

    partial, payload = lax.optimization_barrier((partial, payload))
    base = half(0, partial)
    base, top = lax.optimization_barrier((base, top))
    flat = lambda x: x.reshape(points // LANES, LANES)
    imposed, rate = pl.pallas_call(
        fault_kernel,
        in_specs=whole(9),
        out_specs=whole(2),
        out_shape=[shaped((devices * 4, LANES)), shaped((points // LANES, LANES))],
        compiler_params=LIMIT,
        name="fault",
    )(
        local(arrived), top, flat(earlier_sliding_speed), flat(instant_sensitivity_a),
        flat(aging_memory_theta), wm, wp, vm, pair,
    )
    returned = lax.all_to_all(imposed, ("wide", "narrow"), split_axis=0, concat_axis=0, tiled=True)
    base, rate = lax.optimization_barrier((base, rate))
    base = half(2, base)

    advanced = pl.pallas_call(
        finish_kernel,
        in_specs=whole(6, (0, 1), (3,)),
        out_specs=whole(1)[0],
        out_shape=shaped((ROWS, elems)),
        scratch_shapes=[
            pltpu.VMEM((faces_total + 8, LANES), F32),
            pltpu.VMEM((ROWS, elems), F32),
            pltpu.SemaphoreType.DMA((1,)),
        ],
        compiler_params=LIMIT,
        name="finish",
    )(rupture_side_index, rupture_seat_partition, local(returned), base, surface_measure_quotient, ws)
    return advanced, new_temperature, new_pressure, rate.reshape(points)


def solution(mesh):
    split = P(None, ("wide", "narrow"))
    flat = P(("wide", "narrow"))
    return jax.shard_map(
        per_device,
        mesh=mesh,
        in_specs=(split,) * 3 + (P(),) * 10 + (split,) * 2 + (flat,) * 3 + (split,) * 2 + (flat,) * 2,
        out_specs=(split, split, split, flat),
        check_vma=False,
    )
```

```python
import jax
import jax.numpy as jnp
import numpy as np
from jax import lax
from jax.experimental import pallas as pl
from jax.experimental.pallas import tpu as pltpu
from jax.sharding import PartitionSpec as P

NEWTON = 4
Q, NB, NJ, NG = 9, 20, 10, 16
LANES = 128
ROWS = Q * NB
PAD = 192
HIGHEST = lax.Precision.HIGHEST
F32 = jnp.float32
BF16 = jnp.bfloat16
VMEM = pltpu.MemorySpace.VMEM
SMEM = pltpu.MemorySpace.SMEM
LIMIT = pltpu.CompilerParams(vmem_limit_bytes=56 * 1024 * 1024)


def tables():
    e = np.zeros((ROWS, Q), np.float32)
    f = np.zeros((ROWS, NB), np.float32)
    for q in range(Q):
        for b in range(NB):
            e[q * NB + b, q] = 1
            f[q * NB + b, b] = 1
    g = np.zeros((LANES, Q), np.float32)
    h = np.zeros((LANES, NJ), np.float32)
    for q in range(Q):
        for j in range(NJ):
            g[q * NJ + j, q] = 1
            h[q * NJ + j, j] = 1
    tile = np.zeros((LANES, NG), np.float32)
    for lane in range(LANES):
        tile[lane, lane % NG] = 1
    side = np.zeros((LANES, 4), np.float32)
    for q, column, low, high in ((3, 0, 0.5, 0.5), (6, 0, -0.5, 0.5), (0, 1, 0.5, 0.5), (7, 1, -0.5, 0.5)):
        side[q * NJ : (q + 1) * NJ, column] = low
        side[q * NJ : (q + 1) * NJ, 2 + column] = high
    mid = np.zeros((2, Q, Q), np.float32)
    mid[:] = 0.5 * np.eye(Q)
    mid[0, 6, 3] = -0.5
    mid[1, 6, 3] = 0.5
    linear = np.stack([g @ mid[0] @ g.T, g @ mid[1] @ g.T])
    slip = np.zeros((1, LANES), np.float32)
    slip[0, 3 * NJ : 4 * NJ] = -1.0
    slip[0, 6 * NJ : 7 * NJ] = 0.5
    pair = np.zeros((64, LANES), np.float32)
    for s in range(LANES):
        pair[s // 2, s] = 1
    return e, f, g, h, tile, side, linear, slip, pair


def dot(a, b, ca=1, cb=0, precision=HIGHEST):
    return lax.dot_general(
        a, b, (((ca,), (cb,)), ((), ())), precision=precision, preferred_element_type=F32
    )


def halves(x):
    high = x.astype(BF16)
    return high, (x - high.astype(F32)).astype(BF16)


def single(a, b, cb=0):
    return lax.dot_general(a, b, (((1,), (cb,)), ((), ())), preferred_element_type=F32)


def triple(a, b):
    ah, al = halves(a)
    bh, bl = halves(b)
    return single(ah, bh) + (single(ah, bl) + single(al, bh))


def put(out, at, value, half):
    high, low = halves(value)
    rows, lanes = value.shape
    out[at[0] + (slice(at[1], at[1] + rows), slice(at[2], at[2] + lanes))] = high
    out[at[0] + (slice(half + at[1], half + at[1] + rows), slice(at[2], at[2] + lanes))] = low


def stacked(weights, x, cb=0):
    xh, xl = halves(x)
    half = weights.shape[0] // 2
    both = single(weights, xh, cb)
    return both[0:half] + (both[half:] + single(weights[0:half], xl, cb))


def spread_rows(select, x):
    xh, xl = halves(x)
    return single(select, xh) + single(select, xl)


def grid_of(rows_of, x, lanes_of):
    return spread_rows(rows_of, dot(x, lanes_of, 1, 1))


def prepare_kernel(a, pd, rs, e, f, g, h, mp, wt):
    e_, f_, g_, h_ = e[...], f[...], g[...], h[...]
    eb, fb = e_.astype(BF16), f_.astype(BF16)
    mp[...] = jnp.zeros(mp.shape, BF16)
    for d in range(3):
        left = grid_of(eb, a[:, d, :], e_)
        put(mp, ((), d * PAD, 0), -left * grid_of(fb, pd[d], f_), 3 * PAD)
    same = single(eb, g_.astype(BF16), 1)
    for face in range(4):
        lift = spread_rows(fb, dot(rs[:, face, :], h_, 0, 1))
        high, low = halves(same * lift)
        wt[0, :, face * LANES : (face + 1) * LANES] = high
        wt[1, :, face * LANES : (face + 1) * LANES] = low


def prepare_rest_kernel(
    face, area, sr, rt, bp, qg, e, f, g, h, tile, side, linear, slip,
    open_area, wf, ws, wm, wp, vm,
):
    e_, f_, g_, h_ = e[...], f[...], g[...], h[...]
    eb, fb = e_.astype(BF16), f_.astype(BF16)
    index = face[...]
    high = lax.shift_right_arithmetic(index, 7)
    rows = lax.broadcasted_iota(jnp.int32, (64, index.shape[1]), 0)
    lanes = lax.broadcasted_iota(jnp.int32, (LANES, index.shape[1]), 0)
    upper = jnp.where(rows == high, 1.0, 0.0).astype(BF16)
    lower = jnp.where(lanes == (index & 127), 1.0, 0.0).astype(BF16)
    closed = single(upper, lower, 1)
    for r in range(64):
        at = (slice(r // 16, r // 16 + 1), slice(r % 16 * LANES, (r % 16 + 1) * LANES))
        open_area[at] = jnp.where(closed[r : r + 1] > 0.5, 0.0, area[at])
    wf[...] = jnp.zeros(wf.shape, BF16)
    ws[...] = jnp.zeros(ws.shape, BF16)
    r0 = grid_of(eb, rt[:, 0, :], g_)
    r1 = grid_of(eb, rt[:, 1, :], g_)
    for n in range(4):
        lift = spread_rows(fb, dot(sr[:, n, :], h_, 0, 1))
        put(wf, ((n,), 0, 0), r0 * lift, PAD)
        put(wf, ((n,), 0, LANES), r1 * lift, PAD)
        put(ws, ((n,), 0, 0), (r0 + r1) * lift, PAD)
    hb = dot(dot(h_, bp[...], 1, 1), tile[...], 1, 1)
    hch = dot(dot(h_, dot(bp[...], qg[...], 0, 0)), h_, 1, 1)
    for out, at in ((wm, 0), (wp, 1)):
        out[:, 0:LANES] = hb * side[:, 2 * at : 2 * at + 1]
        out[:, LANES : 2 * LANES] = hb * side[:, 2 * at + 1 : 2 * at + 2]
        out[:, 2 * LANES :] = hch * linear[at]
    vm[...] = dot(dot(tile[...], qg[...]), h_, 1, 1) * slip[...]


def directional(weights, x, times):
    y = stacked(weights, x)
    return (
        y[0:ROWS] * times[0:1]
        + y[PAD : PAD + ROWS] * times[1:2]
        + y[2 * PAD : 2 * PAD + ROWS] * times[2:3]
    )


def predictor_kernel(u, t, a, pd, rs, e, f, g, h, integral, faces, padded, mp, wt):
    @pl.when(pl.program_id(0) == 0)
    def _():
        prepare_kernel(a, pd, rs, e, f, g, h, mp, wt)

    times = t[...]
    current = u[...]
    total = current
    factor = 1.0
    for degree in range(1, 4):
        current = directional(mp[...], current, times)
        factor = factor * (degree + 1)
        total = total + current * (1.0 / factor)
    integral[...] = total
    padded[...] = jnp.zeros(padded.shape, F32)
    padded[0:ROWS, :] = total
    xh, xl = halves(padded[...].T[:, 0:ROWS])
    rows = single(xh, wt[0]) + (single(xh, wt[1]) + single(xl, wt[0]))
    for face in range(4):
        faces[face] = rows[:, face * LANES : (face + 1) * LANES]


def volume_kernel(u, t, integral, a, kd, e, f, partial, mi):
    @pl.when(pl.program_id(0) == 0)
    def _():
        e_, f_ = e[...], f[...]
        eb, fb = e_.astype(BF16), f_.astype(BF16)
        mi[...] = jnp.zeros(mi.shape, BF16)
        for d in range(3):
            left = grid_of(eb, a[:, d, :], e_)
            put(mi, ((), d * PAD, 0), left * grid_of(fb, kd[d], f_), 3 * PAD)

    partial[...] = u[...] + directional(mi[...], integral[...], t[...])


def take_rows(index, row, source, target, base):
    def body(i, carry):
        first = pl.multiple_of(i * LANES, LANES)
        listed = index.at[row, pl.ds(first, LANES)]
        place = target.at[pl.ds(base + first, LANES)]
        for at in range(0, LANES, 16):
            rows = [source[pl.ds(listed[at + k], 1), :] for k in range(16)]
            for k in range(16):
                place[at + k : at + k + 1, :] = rows[k]
        return carry

    lax.fori_loop(0, index.shape[1] // LANES, body, 0)


def send_kernel(index, faces, group, lower, upper):
    for peer in range(4):
        take_rows(index, peer, faces, group, peer * index.shape[1])
    take_rows(index, 4, faces, lower, 0)
    take_rows(index, 5, faces, upper, 0)


def thermal_kernel(th, fl, speed, shape, tr, hr, new_th, new_fl, top):
    v = speed[...]
    old = th[...]
    warmed = old + shape[...] * (0.5 * v * v)
    fresh = stacked(jnp.concatenate(halves(tr[...]), axis=0), warmed)
    new_th[...] = fresh
    pressure = stacked(jnp.concatenate(halves(hr[...]), axis=0), fl[...] + 0.5 * (fresh - old))
    new_fl[...] = pressure
    for r in range(top.shape[0]):
        top[r : r + 1, :] = pressure[0:1, r * LANES : (r + 1) * LANES]


def fill(table, parts, sems):
    at = 0
    copies = []
    for i, part in enumerate(parts):
        rows = part.shape[0]
        copies.append(pltpu.make_async_copy(part, table.at[pl.ds(at, rows)], sems.at[i]))
        at += rows
    for copy in copies:
        copy.start()
    for copy in copies:
        copy.wait()


def live_blocks(seat):
    return lax.fori_loop(
        0, seat.shape[0] // 4, lambda i, c: c + (seat[i * 4] >= 0).astype(jnp.int32), 0
    )


def payload_kernel(face, seat, entry, faces, group, lower, upper, payload, buffer, table, sems):
    extent = table.shape[0] - 8
    buffer[...] = jnp.zeros(buffer.shape, F32)
    table[extent : extent + 8, :] = jnp.zeros((8, LANES), F32)
    blocks = live_blocks(seat)
    fill(table, (faces, group, lower, upper), sems)
    spare = buffer.shape[0] - 8

    def body(i, carry):
        rows = []
        for k in range(16):
            column = face[i * 16 + k]
            live = column >= 0
            safe = jnp.maximum(column, 0)
            outer = entry[lax.shift_right_logical(safe, 11), safe & 2047]
            rows.append(table[pl.ds(jnp.where(live, column, extent), 1), :])
            rows.append(table[pl.ds(jnp.where(live, outer, extent), 1), :])
        for n in range(4):
            owner = seat[i * 16 + n * 4]
            first = jnp.where(owner >= 0, owner * 8, spare)
            for k in range(4):
                buffer[pl.ds(first + k, 1), :] = rows[8 * n + 2 * k]
                buffer[pl.ds(first + 4 + k, 1), :] = rows[8 * n + 2 * k + 1]
        return carry

    lax.fori_loop(0, lax.shift_right_logical(blocks + 3, 2), body, 0)
    copy = pltpu.make_async_copy(buffer.at[pl.ds(0, spare)], payload, sems.at[0])
    copy.start()
    copy.wait()


def outside_kernel(
    first, entry, faces, group, lower, upper, partial, area, wf, base,
    table, outside, held, weights, sems, others,
):
    copies = (
        pltpu.make_async_copy(wf.at[pl.ds(first, 2)], weights, others.at[0]),
        pltpu.make_async_copy(partial, held, others.at[1]),
    )
    fill(table, (faces, group, lower, upper), sems)
    for copy in copies:
        copy.start()
    elems = outside.shape[0]
    result = None
    for n in range(2):
        face = first + n
        take_rows(entry, face, table, outside, 0)
        rows = jnp.concatenate([table[face * elems : (face + 1) * elems, :], outside[...]], axis=1)
        if n == 0:
            for copy in copies:
                copy.wait()
            result = held[...]
        flux = stacked(weights[n], rows, 1)
        result = result - flux[0:ROWS] * area[face : face + 1, :]
    base[...] = result


def fault_kernel(arrived, top, speed, sense, memory, wm, wp, vm, pair, imposed, rate):
    lanes = lax.shift_right_logical(lax.broadcasted_iota(jnp.int32, (LANES, LANES), 1), 4)
    half = (lax.broadcasted_iota(jnp.int32, (LANES, LANES), 0) & 1) * 4
    pick = lambda at: jnp.concatenate(
        [arrived[pl.ds(at + k, LANES, stride=8), :] for k in range(4)], axis=0
    )
    linear = triple(pick(0), wm[...]) + triple(pick(4), wp[...])
    locked = jnp.zeros((LANES, LANES), F32)
    normal = jnp.zeros((LANES, LANES), F32)
    for k in range(4):
        mine = lanes == half + k
        part = linear[k * LANES : (k + 1) * LANES]
        locked = locked + jnp.where(mine, part[:, 0:LANES], 0.0)
        normal = normal + jnp.where(mine, part[:, LANES : 2 * LANES], 0.0)
    locked = dot(pair[...], locked)
    normal = dot(pair[...], normal)
    excess = 2.0 + normal - top[...]
    effective = jnp.maximum(excess, 0.0) + jnp.log1p(jnp.exp(-jnp.abs(excess)))
    strength = effective * sense[...]
    weight = 0.5 * jnp.exp(memory[...] / sense[...])
    v = speed[...]
    for _ in range(NEWTON):
        scaled = weight * v
        root = jnp.sqrt(1.0 + scaled * scaled)
        size = jnp.log(jnp.abs(scaled) + root)
        mismatch = locked - v - strength * jnp.where(scaled < 0.0, -size, size)
        slope = -1.0 - strength * weight / root
        v = v - mismatch / slope
    rate[...] = v
    spread = dot(pair[...], v, 0, 0)
    mine = jnp.concatenate(
        [jnp.where(lanes == half + k, spread, 0.0) for k in range(4)], axis=0
    )
    result = linear[:, 2 * LANES :] + triple(mine, vm[...])
    for k in range(4):
        imposed[pl.ds(k, LANES, stride=4), :] = result[k * LANES : (k + 1) * LANES]


def finish_kernel(face, seat, returned, base, area, ws, out, spread, held, sems):
    copy = pltpu.make_async_copy(base, held, sems.at[0])
    copy.start()
    count = spread.shape[0] - 8
    elems = count // 4
    spread[...] = jnp.zeros(spread.shape, F32)

    def body(i, carry):
        rows = []
        for n in range(4):
            owner = jnp.maximum(seat[i * 16 + n * 4], 0)
            rows += [returned[pl.ds(owner * 4 + k, 1), :] for k in range(4)]
        for k in range(16):
            column = face[i * 16 + k]
            spread[pl.ds(jnp.where(column >= 0, column, count), 1), :] = rows[k]
        return carry

    lax.fori_loop(0, lax.shift_right_logical(live_blocks(seat) + 3, 2), body, 0)
    copy.wait()
    result = held[...]
    for at in range(4):
        flux = stacked(ws[at], spread[at * elems : (at + 1) * elems, :], 1)
        result = result - flux[0:ROWS] * area[at : at + 1, :]
    out[...] = result


def shaped(shape, dtype=F32):
    return jax.ShapeDtypeStruct(shape, dtype)


def whole(count, smem=(), left=()):
    space = lambda i: SMEM if i in smem else pl.ANY if i in left else VMEM
    return [pl.BlockSpec(memory_space=space(i)) for i in range(count)]


def shift(array, axis, by):
    peers = lax.axis_size(axis)
    pairs = [(i, i + by) for i in range(peers) if 0 <= i + by < peers]
    return lax.ppermute(array, axis, pairs)


def per_device(
    modal_unknowns,
    timestep_metric_scaling,
    surface_measure_quotient,
    elastic_directional_derivs,
    predictor_derivatives,
    interior_gradient_tables,
    interior_restriction,
    surface_raise_tables,
    riemann_numerical_tables,
    boundary_polynomials_sampled,
    quadrature_gather_weights,
    thermal_diffusion_resolvent,
    hydraulic_diffusion_resolvent,
    thermal_field,
    fluid_load,
    earlier_sliding_speed,
    instant_sensitivity_a,
    aging_memory_theta,
    outbound_ghost_indices,
    boundary_entry_index,
    rupture_side_index,
    rupture_seat_partition,
):
    elems = modal_unknowns.shape[1]
    faces_total = 4 * elems
    devices = lax.axis_size(("wide", "narrow"))
    points = thermal_field.shape[1]
    e, f, g, h, tile, side, linear, slip, pair = tables()
    entry = boundary_entry_index
    elastic = jnp.transpose(elastic_directional_derivs, (1, 0, 2))

    step = 512
    column = lambda rows: pl.BlockSpec((rows, step), lambda i: (0, i))
    fixed = lambda shape: pl.BlockSpec(shape, lambda i: (0,) * len(shape))
    integral, face_rows = pl.pallas_call(
        predictor_kernel,
        grid=(elems // step,),
        in_specs=[
            column(ROWS), column(3), fixed((Q, 3, Q)), fixed((3, NB, NB)), fixed((NJ, 4, NB)),
            fixed((ROWS, Q)), fixed((ROWS, NB)), fixed((LANES, Q)), fixed((LANES, NJ)),
        ],
        out_specs=[column(ROWS), pl.BlockSpec((4, step, LANES), lambda i: (0, i, 0))],
        out_shape=[shaped((ROWS, elems)), shaped((4, elems, LANES))],
        scratch_shapes=[
            pltpu.VMEM((256, step), F32),
            pltpu.VMEM((6 * PAD, ROWS), BF16),
            pltpu.VMEM((2, ROWS, 4 * LANES), BF16),
        ],
        compiler_params=LIMIT,
        name="predictor",
    )(
        modal_unknowns, timestep_metric_scaling, elastic, predictor_derivatives,
        jnp.transpose(interior_restriction, (1, 0, 2)), e, f, g, h,
    )
    face_rows = face_rows.reshape(faces_total, LANES)

    group_out, lower_out, upper_out = pl.pallas_call(
        send_kernel,
        in_specs=whole(2, (0,)),
        out_specs=whole(3),
        out_shape=[shaped((2048, LANES)), shaped((512, LANES)), shaped((512, LANES))],
        compiler_params=LIMIT,
        name="halo_rows",
    )(outbound_ghost_indices, face_rows)
    group = lax.all_to_all(group_out, "narrow", split_axis=0, concat_axis=0, tiled=True)
    lower = shift(lower_out, "wide", 1)
    upper = shift(upper_out, "wide", -1)

    tensors, sensitivity, _ = lax.optimization_barrier(
        (riemann_numerical_tables, thermal_diffusion_resolvent, lower_out)
    )
    open_area, wf, ws, wm, wp, vm = pl.pallas_call(
        prepare_rest_kernel,
        in_specs=whole(14),
        out_specs=whole(6),
        out_shape=[
            shaped((4, elems)),
            shaped((4, 2 * PAD, 2 * LANES), BF16),
            shaped((4, 2 * PAD, LANES), BF16),
            shaped((LANES, 3 * LANES)),
            shaped((LANES, 3 * LANES)),
            shaped((LANES, LANES)),
        ],
        compiler_params=LIMIT,
        name="prepare_rest",
    )(
        rupture_side_index.reshape(1, -1),
        surface_measure_quotient,
        jnp.transpose(surface_raise_tables, (2, 0, 1)),
        jnp.transpose(tensors, (1, 0, 2)),
        boundary_polynomials_sampled,
        quadrature_gather_weights,
        e, f, g, h, tile, side, linear, slip,
    )

    width = 2048
    block = pl.BlockSpec((64, width), lambda i: (0, i))
    depth = np.arange(64, dtype=np.float32) / 8.0
    curve = np.exp(-depth * depth)[:, None].astype(np.float32)
    new_temperature, new_pressure, top = pl.pallas_call(
        thermal_kernel,
        grid=(points // width,),
        in_specs=[
            block, block, pl.BlockSpec((1, width), lambda i: (0, i)),
            fixed((64, 1)), fixed((64, 64)), fixed((64, 64)),
        ],
        out_specs=[block, block, pl.BlockSpec((width // LANES, LANES), lambda i: (i, 0))],
        out_shape=[shaped((64, points)), shaped((64, points)), shaped((points // LANES, LANES))],
        compiler_params=LIMIT,
        name="thermal",
    )(
        thermal_field, fluid_load, earlier_sliding_speed.reshape(1, points), curve,
        sensitivity, hydraulic_diffusion_resolvent,
    )

    partial = pl.pallas_call(
        volume_kernel,
        grid=(elems // step,),
        in_specs=[
            column(ROWS), column(3), column(ROWS), fixed((Q, 3, Q)), fixed((3, NB, NB)),
            fixed((ROWS, Q)), fixed((ROWS, NB)),
        ],
        scratch_shapes=[pltpu.VMEM((6 * PAD, ROWS), BF16)],
        out_specs=column(ROWS),
        out_shape=shaped((ROWS, elems)),
        compiler_params=LIMIT,
        name="volume",
    )(
        modal_unknowns, timestep_metric_scaling, integral, elastic, interior_gradient_tables, e, f
    )

    faults, partial, top = lax.optimization_barrier((rupture_side_index, partial, top))
    extent = faces_total + 3072
    payload = pl.pallas_call(
        payload_kernel,
        in_specs=whole(7, (0, 1, 2), (3, 4, 5, 6)),
        out_specs=whole(1, (), (0,))[0],
        out_shape=shaped((devices * 8, LANES)),
        scratch_shapes=[
            pltpu.VMEM((devices * 8 + 8, LANES), F32),
            pltpu.VMEM((extent + 8, LANES), F32),
            pltpu.SemaphoreType.DMA((4,)),
        ],
        compiler_params=LIMIT,
        name="payload",
    )(faults, rupture_seat_partition, entry, face_rows, group, lower, upper)
    arrived = lax.all_to_all(payload, ("wide", "narrow"), split_axis=0, concat_axis=0, tiled=True)

    def half(first, value):
        return pl.pallas_call(
            lambda *refs: outside_kernel(first, *refs),
            in_specs=whole(8, (0,), (1, 2, 3, 4, 5, 7)),
            out_specs=whole(1)[0],
            out_shape=shaped((ROWS, elems)),
            scratch_shapes=[
                pltpu.VMEM((extent, LANES), F32),
                pltpu.VMEM((elems, LANES), F32),
                pltpu.VMEM((ROWS, elems), F32),
                pltpu.VMEM((2, 2 * PAD, 2 * LANES), BF16),
                pltpu.SemaphoreType.DMA((4,)),
                pltpu.SemaphoreType.DMA((2,)),
            ],
            compiler_params=LIMIT,
            name="outside" + str(first),
        )(entry, face_rows, group, lower, upper, value, open_area, wf)

    partial, payload = lax.optimization_barrier((partial, payload))
    base = half(0, partial)
    base, top = lax.optimization_barrier((base, top))
    flat = lambda x: x.reshape(points // LANES, LANES)
    imposed, rate = pl.pallas_call(
        fault_kernel,
        in_specs=whole(9),
        out_specs=whole(2),
        out_shape=[shaped((devices * 4, LANES)), shaped((points // LANES, LANES))],
        compiler_params=LIMIT,
        name="fault",
    )(
        arrived, top, flat(earlier_sliding_speed), flat(instant_sensitivity_a),
        flat(aging_memory_theta), wm, wp, vm, pair,
    )
    returned = lax.all_to_all(imposed, ("wide", "narrow"), split_axis=0, concat_axis=0, tiled=True)
    base, rate = lax.optimization_barrier((base, rate))
    base = half(2, base)

    advanced = pl.pallas_call(
        finish_kernel,
        in_specs=whole(6, (0, 1), (3,)),
        out_specs=whole(1)[0],
        out_shape=shaped((ROWS, elems)),
        scratch_shapes=[
            pltpu.VMEM((faces_total + 8, LANES), F32),
            pltpu.VMEM((ROWS, elems), F32),
            pltpu.SemaphoreType.DMA((1,)),
        ],
        compiler_params=LIMIT,
        name="finish",
    )(rupture_side_index, rupture_seat_partition, returned, base, surface_measure_quotient, ws)
    return advanced, new_temperature, new_pressure, rate.reshape(points)


def solution(mesh):
    split = P(None, ("wide", "narrow"))
    flat = P(("wide", "narrow"))
    return jax.shard_map(
        per_device,
        mesh=mesh,
        in_specs=(split,) * 3 + (P(),) * 10 + (split,) * 2 + (flat,) * 3 + (split,) * 2 + (flat,) * 2,
        out_specs=(split, split, split, flat),
        check_vma=False,
    )
```

```python
import jax
import jax.numpy as jnp
import numpy as np
from jax import lax
from jax.experimental import pallas as pl
from jax.experimental.pallas import tpu as pltpu
from jax.sharding import PartitionSpec as P

NEWTON = 4
Q, NB, NJ, NG = 9, 20, 10, 16
LANES = 128
ROWS = Q * NB
PAD = 192
HIGHEST = lax.Precision.HIGHEST
F32 = jnp.float32
BF16 = jnp.bfloat16
VMEM = pltpu.MemorySpace.VMEM
SMEM = pltpu.MemorySpace.SMEM
LIMIT = pltpu.CompilerParams(vmem_limit_bytes=56 * 1024 * 1024)


def tables():
    e = np.zeros((ROWS, Q), np.float32)
    f = np.zeros((ROWS, NB), np.float32)
    for q in range(Q):
        for b in range(NB):
            e[q * NB + b, q] = 1
            f[q * NB + b, b] = 1
    g = np.zeros((LANES, Q), np.float32)
    h = np.zeros((LANES, NJ), np.float32)
    for q in range(Q):
        for j in range(NJ):
            g[q * NJ + j, q] = 1
            h[q * NJ + j, j] = 1
    tile = np.zeros((LANES, NG), np.float32)
    for lane in range(LANES):
        tile[lane, lane % NG] = 1
    side = np.zeros((LANES, 4), np.float32)
    for q, column, low, high in ((3, 0, 0.5, 0.5), (6, 0, -0.5, 0.5), (0, 1, 0.5, 0.5), (7, 1, -0.5, 0.5)):
        side[q * NJ : (q + 1) * NJ, column] = low
        side[q * NJ : (q + 1) * NJ, 2 + column] = high
    mid = np.zeros((2, Q, Q), np.float32)
    mid[:] = 0.5 * np.eye(Q)
    mid[0, 6, 3] = -0.5
    mid[1, 6, 3] = 0.5
    linear = np.stack([g @ mid[0] @ g.T, g @ mid[1] @ g.T])
    slip = np.zeros((1, LANES), np.float32)
    slip[0, 3 * NJ : 4 * NJ] = -1.0
    slip[0, 6 * NJ : 7 * NJ] = 0.5
    pair = np.zeros((64, LANES), np.float32)
    for s in range(LANES):
        pair[s // 2, s] = 1
    return e, f, g, h, tile, side, linear, slip, pair


def dot(a, b, ca=1, cb=0, precision=HIGHEST):
    return lax.dot_general(
        a, b, (((ca,), (cb,)), ((), ())), precision=precision, preferred_element_type=F32
    )


def halves(x):
    high = x.astype(BF16)
    return high, (x - high.astype(F32)).astype(BF16)


def single(a, b, cb=0):
    return lax.dot_general(a, b, (((1,), (cb,)), ((), ())), preferred_element_type=F32)


def triple(a, b):
    ah, al = halves(a)
    bh, bl = halves(b)
    return single(ah, bh) + (single(ah, bl) + single(al, bh))


def put(out, at, value, half):
    high, low = halves(value)
    rows, lanes = value.shape
    out[at[0] + (slice(at[1], at[1] + rows), slice(at[2], at[2] + lanes))] = high
    out[at[0] + (slice(half + at[1], half + at[1] + rows), slice(at[2], at[2] + lanes))] = low


def stacked(weights, x, cb=0):
    xh, xl = halves(x)
    half = weights.shape[0] // 2
    both = single(weights, xh, cb)
    return both[0:half] + (both[half:] + single(weights[0:half], xl, cb))


def spread_rows(select, x):
    xh, xl = halves(x)
    return single(select, xh) + single(select, xl)


def grid_of(rows_of, x, lanes_of):
    return spread_rows(rows_of, dot(x, lanes_of, 1, 1))


def prepare_kernel(a, pd, rs, e, f, g, h, mp, wt):
    e_, f_, g_, h_ = e[...], f[...], g[...], h[...]
    eb, fb = e_.astype(BF16), f_.astype(BF16)
    mp[...] = jnp.zeros(mp.shape, BF16)
    for d in range(3):
        left = grid_of(eb, a[:, d, :], e_)
        put(mp, ((), d * PAD, 0), -left * grid_of(fb, pd[d], f_), 3 * PAD)
    same = single(eb, g_.astype(BF16), 1)
    for face in range(4):
        lift = spread_rows(fb, dot(rs[:, face, :], h_, 0, 1))
        high, low = halves(same * lift)
        wt[0, :, face * LANES : (face + 1) * LANES] = high
        wt[1, :, face * LANES : (face + 1) * LANES] = low


def prepare_rest_kernel(
    face, area, sr, rt, bp, qg, e, f, g, h, tile, side, linear, slip,
    open_area, wf, ws, wm, wp, vm,
):
    e_, f_, g_, h_ = e[...], f[...], g[...], h[...]
    eb, fb = e_.astype(BF16), f_.astype(BF16)
    index = face[...]
    high = lax.shift_right_arithmetic(index, 7)
    rows = lax.broadcasted_iota(jnp.int32, (64, index.shape[1]), 0)
    lanes = lax.broadcasted_iota(jnp.int32, (LANES, index.shape[1]), 0)
    upper = jnp.where(rows == high, 1.0, 0.0).astype(BF16)
    lower = jnp.where(lanes == (index & 127), 1.0, 0.0).astype(BF16)
    closed = single(upper, lower, 1)
    for r in range(64):
        at = (slice(r // 16, r // 16 + 1), slice(r % 16 * LANES, (r % 16 + 1) * LANES))
        open_area[at] = jnp.where(closed[r : r + 1] > 0.5, 0.0, area[at])
    wf[...] = jnp.zeros(wf.shape, BF16)
    ws[...] = jnp.zeros(ws.shape, BF16)
    r0 = grid_of(eb, rt[:, 0, :], g_)
    r1 = grid_of(eb, rt[:, 1, :], g_)
    for n in range(4):
        lift = spread_rows(fb, dot(sr[:, n, :], h_, 0, 1))
        put(wf, ((n,), 0, 0), r0 * lift, PAD)
        put(wf, ((n,), 0, LANES), r1 * lift, PAD)
        put(ws, ((n,), 0, 0), (r0 + r1) * lift, PAD)
    hb = dot(dot(h_, bp[...], 1, 1), tile[...], 1, 1)
    hch = dot(dot(h_, dot(bp[...], qg[...], 0, 0)), h_, 1, 1)
    for out, at in ((wm, 0), (wp, 1)):
        out[:, 0:LANES] = hb * side[:, 2 * at : 2 * at + 1]
        out[:, LANES : 2 * LANES] = hb * side[:, 2 * at + 1 : 2 * at + 2]
        out[:, 2 * LANES :] = hch * linear[at]
    vm[...] = dot(dot(tile[...], qg[...]), h_, 1, 1) * slip[...]


def directional(weights, x, times):
    y = stacked(weights, x)
    return (
        y[0:ROWS] * times[0:1]
        + y[PAD : PAD + ROWS] * times[1:2]
        + y[2 * PAD : 2 * PAD + ROWS] * times[2:3]
    )


def take_rows(index, row, source, target, base):
    def body(i, carry):
        first = pl.multiple_of(i * LANES, LANES)
        listed = index.at[row, pl.ds(first, LANES)]
        place = target.at[pl.ds(base + first, LANES)]
        for at in range(0, LANES, 16):
            rows = [source[pl.ds(listed[at + k], 1), :] for k in range(16)]
            for k in range(16):
                place[at + k : at + k + 1, :] = rows[k]
        return carry

    lax.fori_loop(0, index.shape[1] // LANES, body, 0)


def send_kernel(index, faces, group, lower, upper):
    for peer in range(4):
        take_rows(index, peer, faces, group, peer * index.shape[1])
    take_rows(index, 4, faces, lower, 0)
    take_rows(index, 5, faces, upper, 0)


def predictor_kernel(
    u, t, a, pd, rs, e, f, g, h, index,
    integral, faces, group, lower, upper, padded, mp, wt, traces,
):
    @pl.when(pl.program_id(0) == 0)
    def _():
        prepare_kernel(a, pd, rs, e, f, g, h, mp, wt)

    times = t[...]
    current = u[...]
    total = current
    factor = 1.0
    for degree in range(1, 4):
        current = directional(mp[...], current, times)
        factor = factor * (degree + 1)
        total = total + current * (1.0 / factor)
    integral[...] = total
    padded[...] = jnp.zeros(padded.shape, F32)
    padded[0:ROWS, :] = total
    xh, xl = halves(padded[...].T[:, 0:ROWS])
    rows = single(xh, wt[0]) + (single(xh, wt[1]) + single(xl, wt[0]))
    for face in range(4):
        block = rows[:, face * LANES : (face + 1) * LANES]
        faces[face] = block
        step = block.shape[0]
        first = face * (traces.shape[0] // 4) + pl.program_id(0) * step
        traces[pl.ds(pl.multiple_of(first, step), step), :] = block

    @pl.when(pl.program_id(0) == pl.num_programs(0) - 1)
    def _():
        send_kernel(index, traces, group, lower, upper)


def volume_kernel(u, t, integral, a, kd, e, f, partial, mi):
    @pl.when(pl.program_id(0) == 0)
    def _():
        e_, f_ = e[...], f[...]
        eb, fb = e_.astype(BF16), f_.astype(BF16)
        mi[...] = jnp.zeros(mi.shape, BF16)
        for d in range(3):
            left = grid_of(eb, a[:, d, :], e_)
            put(mi, ((), d * PAD, 0), left * grid_of(fb, kd[d], f_), 3 * PAD)

    partial[...] = u[...] + directional(mi[...], integral[...], t[...])


def thermal_kernel(th, fl, speed, shape, tr, hr, new_th, new_fl, top):
    v = speed[...]
    old = th[...]
    warmed = old + shape[...] * (0.5 * v * v)
    fresh = stacked(jnp.concatenate(halves(tr[...]), axis=0), warmed)
    new_th[...] = fresh
    pressure = stacked(jnp.concatenate(halves(hr[...]), axis=0), fl[...] + 0.5 * (fresh - old))
    new_fl[...] = pressure
    for r in range(top.shape[0]):
        top[r : r + 1, :] = pressure[0:1, r * LANES : (r + 1) * LANES]


def fill(table, parts, sems):
    at = 0
    copies = []
    for i, part in enumerate(parts):
        rows = part.shape[0]
        copies.append(pltpu.make_async_copy(part, table.at[pl.ds(at, rows)], sems.at[i]))
        at += rows
    for copy in copies:
        copy.start()
    for copy in copies:
        copy.wait()


def live_blocks(seat):
    return lax.fori_loop(
        0, seat.shape[0] // 4, lambda i, c: c + (seat[i * 4] >= 0).astype(jnp.int32), 0
    )


def payload_kernel(face, seat, entry, faces, group, lower, upper, payload, buffer, table, sems):
    extent = table.shape[0] - 8
    buffer[...] = jnp.zeros(buffer.shape, F32)
    table[extent : extent + 8, :] = jnp.zeros((8, LANES), F32)
    blocks = live_blocks(seat)
    fill(table, (faces, group, lower, upper), sems)
    spare = buffer.shape[0] - 8

    def body(i, carry):
        rows = []
        for k in range(16):
            column = face[i * 16 + k]
            live = column >= 0
            safe = jnp.maximum(column, 0)
            outer = entry[lax.shift_right_logical(safe, 11), safe & 2047]
            rows.append(table[pl.ds(jnp.where(live, column, extent), 1), :])
            rows.append(table[pl.ds(jnp.where(live, outer, extent), 1), :])
        for n in range(4):
            owner = seat[i * 16 + n * 4]
            first = jnp.where(owner >= 0, owner * 8, spare)
            for k in range(4):
                buffer[pl.ds(first + k, 1), :] = rows[8 * n + 2 * k]
                buffer[pl.ds(first + 4 + k, 1), :] = rows[8 * n + 2 * k + 1]
        return carry

    lax.fori_loop(0, lax.shift_right_logical(blocks + 3, 2), body, 0)
    copy = pltpu.make_async_copy(buffer.at[pl.ds(0, spare)], payload, sems.at[0])
    copy.start()
    copy.wait()


def outside_kernel(
    first, entry, faces, group, lower, upper, partial, area, wf, base,
    table, outside, held, weights, sems, others,
):
    copies = (
        pltpu.make_async_copy(wf.at[pl.ds(first, 2)], weights, others.at[0]),
        pltpu.make_async_copy(partial, held, others.at[1]),
    )
    fill(table, (faces, group, lower, upper), sems)
    for copy in copies:
        copy.start()
    elems = outside.shape[0]
    result = None
    for n in range(2):
        face = first + n
        take_rows(entry, face, table, outside, 0)
        rows = jnp.concatenate([table[face * elems : (face + 1) * elems, :], outside[...]], axis=1)
        if n == 0:
            for copy in copies:
                copy.wait()
            result = held[...]
        flux = stacked(weights[n], rows, 1)
        result = result - flux[0:ROWS] * area[face : face + 1, :]
    base[...] = result


def fault_kernel(arrived, top, speed, sense, memory, wm, wp, vm, pair, imposed, rate):
    lanes = lax.shift_right_logical(lax.broadcasted_iota(jnp.int32, (LANES, LANES), 1), 4)
    half = (lax.broadcasted_iota(jnp.int32, (LANES, LANES), 0) & 1) * 4
    pick = lambda at: jnp.concatenate(
        [arrived[pl.ds(at + k, LANES, stride=8), :] for k in range(4)], axis=0
    )
    linear = triple(pick(0), wm[...]) + triple(pick(4), wp[...])
    locked = jnp.zeros((LANES, LANES), F32)
    normal = jnp.zeros((LANES, LANES), F32)
    for k in range(4):
        mine = lanes == half + k
        part = linear[k * LANES : (k + 1) * LANES]
        locked = locked + jnp.where(mine, part[:, 0:LANES], 0.0)
        normal = normal + jnp.where(mine, part[:, LANES : 2 * LANES], 0.0)
    locked = dot(pair[...], locked)
    normal = dot(pair[...], normal)
    excess = 2.0 + normal - top[...]
    effective = jnp.maximum(excess, 0.0) + jnp.log1p(jnp.exp(-jnp.abs(excess)))
    strength = effective * sense[...]
    weight = 0.5 * jnp.exp(memory[...] / sense[...])
    v = speed[...]
    for _ in range(NEWTON):
        scaled = weight * v
        root = jnp.sqrt(1.0 + scaled * scaled)
        size = jnp.log(jnp.abs(scaled) + root)
        mismatch = locked - v - strength * jnp.where(scaled < 0.0, -size, size)
        slope = -1.0 - strength * weight / root
        v = v - mismatch / slope
    rate[...] = v
    spread = dot(pair[...], v, 0, 0)
    mine = jnp.concatenate(
        [jnp.where(lanes == half + k, spread, 0.0) for k in range(4)], axis=0
    )
    result = linear[:, 2 * LANES :] + triple(mine, vm[...])
    for k in range(4):
        imposed[pl.ds(k, LANES, stride=4), :] = result[k * LANES : (k + 1) * LANES]


def finish_kernel(face, seat, returned, base, area, ws, out, spread, held, sems):
    copy = pltpu.make_async_copy(base, held, sems.at[0])
    copy.start()
    count = spread.shape[0] - 8
    elems = count // 4
    spread[...] = jnp.zeros(spread.shape, F32)

    def body(i, carry):
        rows = []
        for n in range(4):
            owner = jnp.maximum(seat[i * 16 + n * 4], 0)
            rows += [returned[pl.ds(owner * 4 + k, 1), :] for k in range(4)]
        for k in range(16):
            column = face[i * 16 + k]
            spread[pl.ds(jnp.where(column >= 0, column, count), 1), :] = rows[k]
        return carry

    lax.fori_loop(0, lax.shift_right_logical(live_blocks(seat) + 3, 2), body, 0)
    copy.wait()
    result = held[...]
    for at in range(4):
        flux = stacked(ws[at], spread[at * elems : (at + 1) * elems, :], 1)
        result = result - flux[0:ROWS] * area[at : at + 1, :]
    out[...] = result


def shaped(shape, dtype=F32):
    return jax.ShapeDtypeStruct(shape, dtype)


def whole(count, smem=(), left=()):
    space = lambda i: SMEM if i in smem else pl.ANY if i in left else VMEM
    return [pl.BlockSpec(memory_space=space(i)) for i in range(count)]


def shift(array, axis, by):
    peers = lax.axis_size(axis)
    pairs = [(i, i + by) for i in range(peers) if 0 <= i + by < peers]
    return lax.ppermute(array, axis, pairs)


def per_device(
    modal_unknowns,
    timestep_metric_scaling,
    surface_measure_quotient,
    elastic_directional_derivs,
    predictor_derivatives,
    interior_gradient_tables,
    interior_restriction,
    surface_raise_tables,
    riemann_numerical_tables,
    boundary_polynomials_sampled,
    quadrature_gather_weights,
    thermal_diffusion_resolvent,
    hydraulic_diffusion_resolvent,
    thermal_field,
    fluid_load,
    earlier_sliding_speed,
    instant_sensitivity_a,
    aging_memory_theta,
    outbound_ghost_indices,
    boundary_entry_index,
    rupture_side_index,
    rupture_seat_partition,
):
    elems = modal_unknowns.shape[1]
    faces_total = 4 * elems
    devices = lax.axis_size(("wide", "narrow"))
    points = thermal_field.shape[1]
    e, f, g, h, tile, side, linear, slip, pair = tables()
    entry = boundary_entry_index
    elastic = jnp.transpose(elastic_directional_derivs, (1, 0, 2))

    step = 512
    column = lambda rows: pl.BlockSpec((rows, step), lambda i: (0, i))
    fixed = lambda shape: pl.BlockSpec(shape, lambda i: (0,) * len(shape))
    integral, face_rows, group_out, lower_out, upper_out = pl.pallas_call(
        predictor_kernel,
        grid=(elems // step,),
        in_specs=[
            column(ROWS), column(3), fixed((Q, 3, Q)), fixed((3, NB, NB)), fixed((NJ, 4, NB)),
            fixed((ROWS, Q)), fixed((ROWS, NB)), fixed((LANES, Q)), fixed((LANES, NJ)),
            pl.BlockSpec(memory_space=SMEM),
        ],
        out_specs=[
            column(ROWS), pl.BlockSpec((4, step, LANES), lambda i: (0, i, 0)),
            fixed((2048, LANES)), fixed((512, LANES)), fixed((512, LANES)),
        ],
        out_shape=[
            shaped((ROWS, elems)), shaped((4, elems, LANES)),
            shaped((2048, LANES)), shaped((512, LANES)), shaped((512, LANES)),
        ],
        scratch_shapes=[
            pltpu.VMEM((256, step), F32),
            pltpu.VMEM((6 * PAD, ROWS), BF16),
            pltpu.VMEM((2, ROWS, 4 * LANES), BF16),
            pltpu.VMEM((faces_total, LANES), F32),
        ],
        compiler_params=LIMIT,
        name="predictor",
    )(
        modal_unknowns, timestep_metric_scaling, elastic, predictor_derivatives,
        jnp.transpose(interior_restriction, (1, 0, 2)), e, f, g, h,
        outbound_ghost_indices,
    )
    face_rows = face_rows.reshape(faces_total, LANES)

    group = lax.all_to_all(group_out, "narrow", split_axis=0, concat_axis=0, tiled=True)
    lower = shift(lower_out, "wide", 1)
    upper = shift(upper_out, "wide", -1)

    tensors, sensitivity, _ = lax.optimization_barrier(
        (riemann_numerical_tables, thermal_diffusion_resolvent, lower_out)
    )
    open_area, wf, ws, wm, wp, vm = pl.pallas_call(
        prepare_rest_kernel,
        in_specs=whole(14),
        out_specs=whole(6),
        out_shape=[
            shaped((4, elems)),
            shaped((4, 2 * PAD, 2 * LANES), BF16),
            shaped((4, 2 * PAD, LANES), BF16),
            shaped((LANES, 3 * LANES)),
            shaped((LANES, 3 * LANES)),
            shaped((LANES, LANES)),
        ],
        compiler_params=LIMIT,
        name="prepare_rest",
    )(
        rupture_side_index.reshape(1, -1),
        surface_measure_quotient,
        jnp.transpose(surface_raise_tables, (2, 0, 1)),
        jnp.transpose(tensors, (1, 0, 2)),
        boundary_polynomials_sampled,
        quadrature_gather_weights,
        e, f, g, h, tile, side, linear, slip,
    )

    width = 2048
    block = pl.BlockSpec((64, width), lambda i: (0, i))
    depth = np.arange(64, dtype=np.float32) / 8.0
    curve = np.exp(-depth * depth)[:, None].astype(np.float32)
    new_temperature, new_pressure, top = pl.pallas_call(
        thermal_kernel,
        grid=(points // width,),
        in_specs=[
            block, block, pl.BlockSpec((1, width), lambda i: (0, i)),
            fixed((64, 1)), fixed((64, 64)), fixed((64, 64)),
        ],
        out_specs=[block, block, pl.BlockSpec((width // LANES, LANES), lambda i: (i, 0))],
        out_shape=[shaped((64, points)), shaped((64, points)), shaped((points // LANES, LANES))],
        compiler_params=LIMIT,
        name="thermal",
    )(
        thermal_field, fluid_load, earlier_sliding_speed.reshape(1, points), curve,
        sensitivity, hydraulic_diffusion_resolvent,
    )

    partial = pl.pallas_call(
        volume_kernel,
        grid=(elems // step,),
        in_specs=[
            column(ROWS), column(3), column(ROWS), fixed((Q, 3, Q)), fixed((3, NB, NB)),
            fixed((ROWS, Q)), fixed((ROWS, NB)),
        ],
        scratch_shapes=[pltpu.VMEM((6 * PAD, ROWS), BF16)],
        out_specs=column(ROWS),
        out_shape=shaped((ROWS, elems)),
        compiler_params=LIMIT,
        name="volume",
    )(
        modal_unknowns, timestep_metric_scaling, integral, elastic, interior_gradient_tables, e, f
    )

    faults, partial, top = lax.optimization_barrier((rupture_side_index, partial, top))
    extent = faces_total + 3072
    payload = pl.pallas_call(
        payload_kernel,
        in_specs=whole(7, (0, 1, 2), (3, 4, 5, 6)),
        out_specs=whole(1, (), (0,))[0],
        out_shape=shaped((devices * 8, LANES)),
        scratch_shapes=[
            pltpu.VMEM((devices * 8 + 8, LANES), F32),
            pltpu.VMEM((extent + 8, LANES), F32),
            pltpu.SemaphoreType.DMA((4,)),
        ],
        compiler_params=LIMIT,
        name="payload",
    )(faults, rupture_seat_partition, entry, face_rows, group, lower, upper)
    arrived = lax.all_to_all(payload, ("wide", "narrow"), split_axis=0, concat_axis=0, tiled=True)

    def half(first, value):
        return pl.pallas_call(
            lambda *refs: outside_kernel(first, *refs),
            in_specs=whole(8, (0,), (1, 2, 3, 4, 5, 7)),
            out_specs=whole(1)[0],
            out_shape=shaped((ROWS, elems)),
            scratch_shapes=[
                pltpu.VMEM((extent, LANES), F32),
                pltpu.VMEM((elems, LANES), F32),
                pltpu.VMEM((ROWS, elems), F32),
                pltpu.VMEM((2, 2 * PAD, 2 * LANES), BF16),
                pltpu.SemaphoreType.DMA((4,)),
                pltpu.SemaphoreType.DMA((2,)),
            ],
            compiler_params=LIMIT,
            name="outside" + str(first),
        )(entry, face_rows, group, lower, upper, value, open_area, wf)

    partial, payload = lax.optimization_barrier((partial, payload))
    base = half(0, partial)
    base, top = lax.optimization_barrier((base, top))
    flat = lambda x: x.reshape(points // LANES, LANES)
    imposed, rate = pl.pallas_call(
        fault_kernel,
        in_specs=whole(9),
        out_specs=whole(2),
        out_shape=[shaped((devices * 4, LANES)), shaped((points // LANES, LANES))],
        compiler_params=LIMIT,
        name="fault",
    )(
        arrived, top, flat(earlier_sliding_speed), flat(instant_sensitivity_a),
        flat(aging_memory_theta), wm, wp, vm, pair,
    )
    returned = lax.all_to_all(imposed, ("wide", "narrow"), split_axis=0, concat_axis=0, tiled=True)
    base, rate = lax.optimization_barrier((base, rate))
    base = half(2, base)

    advanced = pl.pallas_call(
        finish_kernel,
        in_specs=whole(6, (0, 1), (3,)),
        out_specs=whole(1)[0],
        out_shape=shaped((ROWS, elems)),
        scratch_shapes=[
            pltpu.VMEM((faces_total + 8, LANES), F32),
            pltpu.VMEM((ROWS, elems), F32),
            pltpu.SemaphoreType.DMA((1,)),
        ],
        compiler_params=LIMIT,
        name="finish",
    )(rupture_side_index, rupture_seat_partition, returned, base, surface_measure_quotient, ws)
    return advanced, new_temperature, new_pressure, rate.reshape(points)


def solution(mesh):
    split = P(None, ("wide", "narrow"))
    flat = P(("wide", "narrow"))
    return jax.shard_map(
        per_device,
        mesh=mesh,
        in_specs=(split,) * 3 + (P(),) * 10 + (split,) * 2 + (flat,) * 3 + (split,) * 2 + (flat,) * 2,
        out_specs=(split, split, split, flat),
        check_vma=False,
    )
```
